512 devices in a mesh: stack: 4 (over x), pix: 128 (over y, z, core).
Axes of the slice: x: 4, y: 4, z: 16, core: 2. Of those that a mesh axis runs over, the one named last changes fastest.
Arguments:
- slc: bfloat16 [2, 4, 15, 768, 256], P(None, 'stack', None, 'pix'), may hold values from -6 to 6
- owner_map: int32 [128], replicated, may hold values from 0 to 127, each once
Outputs:
- linked: float32 [2, 4, 15, 128, 1536], P(None, 'stack', None, 'pix')
- compressed: float32 [2, 4, 128, 1536], P(None, 'stack', 'pix')
The draws below stay inside these ranges and needn't reach their ends.
Inputs may be any that keep to these rules, and one draw needn't show every extreme that they name: owner_map is a permutation: each owner slot receives exactly one column block.
All inputs are finite; a program needn't handle non-finite values.
Results may differ from the reference program's by a relative error of at most 0.005.
Values may be sent and summed in bfloat16 or wider, within the bound.
A program may use at most 64 MiB of HBM per device.

```python
import math
import jax
import jax.numpy as jnp
import numpy as np
from jax import lax

DATES = 15
ITERS = 8
SECT = 4
ROWS = 768
COLS = 256
BLOCKS = 128


def shard_levels(stream_key, dims, shards, smallest, high):
    factor_of = 1.0
    for dim, blocks in shards:
        steps = jax.random.uniform(jax.random.fold_in(jax.random.fold_in(stream_key, 6), dim), (blocks,), jnp.float32, smallest / len(shards), high / len(shards))
        factor_of = factor_of * jnp.repeat(jnp.exp(steps), dims[dim] // blocks).reshape((-1,) + (1,) * (len(dims) - 1 - dim))
    return factor_of


def normal_values(stream_key, extent, scale, bound, cuts=(), kind=jnp.bfloat16):
    factor_of = shard_levels(stream_key, extent, cuts, -0.22, 0.18) if cuts else 1.0
    array = jax.random.normal(stream_key, extent, jnp.float32) * scale * factor_of
    return jnp.minimum(jnp.maximum(array, -bound), bound).astype(kind)


def setup_inputs(seed: int = 0) -> dict:
    arg_keys = jax.random.split(jax.random.key(seed), 3)
    slc = normal_values(arg_keys[0], (2, SECT, DATES, ROWS, COLS), 1.0, 6.0, ((1, 4), (3, 128)))
    owner_map = jax.random.permutation(arg_keys[1], BLOCKS).astype(jnp.int32)
    return dict(slc=slc, owner_map=owner_map)


def window_sum(values, tall, broad):
    height = values.shape[-2] - tall + 1
    across = values[..., 0:height, :]
    for offset in range(1, tall):
        across = across + values[..., offset:offset + height, :]
    width = values.shape[-1] - broad + 1
    result = across[..., 0:width]
    for offset in range(1, broad):
        result = result + across[..., offset:offset + width]
    return result

def coherence(real_part, imag_part, tall, broad):
    dates = real_part.shape[0]
    first, second = np.triu_indices(dates, 1)
    groups = first.shape[0] // dates
    real_full = real_part.astype(jnp.float32)
    imag_full = imag_part.astype(jnp.float32)
    energy = window_sum(real_full * real_full + imag_full * imag_full, tall, broad) + 1.0

    def one_group(indices):
        left_idx, right_idx = indices
        left_re = real_full[left_idx]
        left_im = imag_full[left_idx]
        right_re = real_full[right_idx]
        right_im = imag_full[right_idx]
        prod_re = left_re * right_re + left_im * right_im
        prod_im = left_im * right_re - left_re * right_im
        scale = lax.rsqrt(energy[left_idx] * energy[right_idx])
        return ((window_sum(prod_re, tall, broad) * scale).astype(jnp.bfloat16), (window_sum(prod_im, tall, broad) * scale).astype(jnp.bfloat16))
    first_groups = jnp.asarray(first.reshape(groups, dates), dtype=jnp.int32)
    second_groups = jnp.asarray(second.reshape(groups, dates), dtype=jnp.int32)
    gamma_re, gamma_im = lax.map(one_group, (first_groups, second_groups))
    return (gamma_re.reshape((-1,) + gamma_re.shape[2:]), gamma_im.reshape((-1,) + gamma_im.shape[2:]))

def hermitian_tables(dates):
    first, second = np.triu_indices(dates, 1)
    npairs = first.shape[0]
    symmetric = np.zeros((dates * dates, npairs), np.float32)
    antisym = np.zeros((dates * dates, npairs), np.float32)
    for index in range(npairs):
        upper = int(first[index]) * dates + int(second[index])
        lower = int(second[index]) * dates + int(first[index])
        symmetric[upper, index] = 1.0
        symmetric[lower, index] = 1.0
        antisym[upper, index] = 1.0
        antisym[lower, index] = -1.0
    diagonal = np.eye(dates, dtype=np.float32).reshape(-1, 1)
    return (symmetric, antisym, diagonal)

def link_block(gamma_re, gamma_im, samples):
    dates = samples.shape[1]
    pixels = samples.shape[2]
    symmetric, antisym, diagonal = hermitian_tables(dates)
    full_re = (jnp.dot(jnp.asarray(symmetric, dtype=jnp.bfloat16), gamma_re, preferred_element_type=jnp.float32) + jnp.asarray(diagonal, dtype=jnp.float32)).astype(jnp.bfloat16).reshape(dates, dates, pixels)
    full_im = jnp.dot(jnp.asarray(antisym, dtype=jnp.bfloat16), gamma_im, preferred_element_type=jnp.float32).astype(jnp.bfloat16).reshape(dates, dates, pixels)
    vec_re = jnp.ones((dates, pixels), jnp.float32)
    vec_im = jnp.zeros((dates, pixels), jnp.float32)
    for count in range(ITERS):
        next_re = lax.optimization_barrier(jnp.sum(full_re * vec_re[None] - full_im * vec_im[None], axis=1))
        next_im = lax.optimization_barrier(jnp.sum(full_re * vec_im[None] + full_im * vec_re[None], axis=1))
        energy = lax.optimization_barrier(jnp.sum(next_re * next_re + next_im * next_im, axis=0)) / dates
        factor = lax.rsqrt(energy + 0.25)
        vec_re = next_re * factor
        vec_im = next_im * factor
    sample_re = samples[0].astype(jnp.float32)
    sample_im = samples[1].astype(jnp.float32)
    norm = 1.0 / math.sqrt(dates)
    packed_re = lax.optimization_barrier(jnp.sum(vec_re * sample_re + vec_im * sample_im, axis=0)) * norm
    packed_im = lax.optimization_barrier(jnp.sum(vec_re * sample_im - vec_im * sample_re, axis=0)) * norm
    return (vec_re, vec_im, packed_re, packed_im)

def to_owner(values, inverse, n_blocks):
    feats = values.shape[0]
    rows_all = values.shape[1]
    width = values.shape[2] // n_blocks
    grid = values.reshape(feats, rows_all, n_blocks, width)
    grid = jnp.take(grid, inverse, axis=2)
    return grid.transpose(2, 0, 3, 1).reshape(n_blocks, feats, width * rows_all)

def reference(slc, owner_map):
    inverse = jnp.argsort(owner_map).astype(jnp.int32)

    def section(stack_slice):
        padded = jnp.pad(stack_slice, ((0, 0), (0, 0), (5, 5), (2, 2)))
        gamma_re, gamma_im = coherence(padded[0], padded[1], 11, 5)
        gathered = to_owner(jnp.concatenate([gamma_re, gamma_im], axis=0), inverse, BLOCKS)
        samples = to_owner(stack_slice.reshape(2 * DATES, ROWS, COLS), inverse, BLOCKS)

        def per_block(pieces):
            gamma_both, owned = pieces
            npairs = gamma_both.shape[0] // 2
            return link_block(gamma_both[:npairs], gamma_both[npairs:], owned.reshape(2, DATES, -1))
        return lax.map(per_block, (gathered, samples))
    vec_re, vec_im, packed_re, packed_im = lax.map(section, jnp.moveaxis(slc, 1, 0))
    datum_re = jnp.ones_like(packed_re[0])
    datum_im = jnp.zeros_like(packed_re[0])
    linked_re = []
    linked_im = []
    for index in range(SECT):
        linked_re.append(vec_re[index] * datum_re[:, None, :] - vec_im[index] * datum_im[:, None, :])
        linked_im.append(vec_re[index] * datum_im[:, None, :] + vec_im[index] * datum_re[:, None, :])
        if index + 1 < SECT:
            link_re = packed_re[index + 1] * packed_re[index] + packed_im[index + 1] * packed_im[index]
            link_im = packed_im[index + 1] * packed_re[index] - packed_re[index + 1] * packed_im[index]
            factor = lax.rsqrt(link_re * link_re + link_im * link_im + 1.0)
            unit_re = link_re * factor
            unit_im = link_im * factor
            datum_re, datum_im = (datum_re * unit_re - datum_im * unit_im, datum_re * unit_im + datum_im * unit_re)
    linked = jnp.stack([jnp.stack(linked_re), jnp.stack(linked_im)]).transpose(0, 1, 3, 2, 4)
    compressed = jnp.stack([packed_re, packed_im])
    return (linked, compressed)
```

```python
import math

import jax
import jax.numpy as jnp
from jax import lax
from jax.experimental import pallas as pl
from jax.experimental.pallas import tpu as pltpu
from jax.sharding import PartitionSpec as P

MESH = pl.DeviceIdType.MESH
F32, BF16, I32 = jnp.float32, jnp.bfloat16, jnp.int32
DATES, ITERS, SECT, ROWS, COLS, BLOCKS = 15, 8, 4, 768, 256, 128
STRIP = 6
UP = 5
TALL = 16
NY, NZ, NC = 4, 16, 2
GROUPS = NY * NC
FEAT = 32
XS = 24
NT_DIMS = (((1,), (1,)), ((), ()))


def place(y, z, c):
    return y * (NZ * NC) + z * NC + c


def halo_kernel(x_ref, out_ref, send_sem, recv_sem):
    me = lax.axis_index("pix")
    count = BLOCKS
    after, before = lax.rem(me + 1, count), lax.rem(me + count - 1, count)
    barrier = pltpu.get_barrier_semaphore()
    for peer in (after, before):
        pl.semaphore_signal(barrier, inc=1, device_id={"pix": peer}, device_id_type=MESH)
    pl.semaphore_wait(barrier, 2)
    copies = []
    for i, peer in enumerate((after, before)):
        copy = pltpu.make_async_remote_copy(
            src_ref=x_ref,
            dst_ref=out_ref.at[i],
            send_sem=send_sem.at[i],
            recv_sem=recv_sem.at[i],
            device_id={"pix": peer},
            device_id_type=MESH,
        )
        copy.start()
        copies.append(copy)
    for copy in copies:
        copy.wait()


def exchange_halo(x):
    return pl.pallas_call(
        halo_kernel,
        out_shape=jax.ShapeDtypeStruct((2,) + x.shape, x.dtype),
        in_specs=[pl.BlockSpec(memory_space=pl.ANY)],
        out_specs=pl.BlockSpec(memory_space=pl.ANY),
        scratch_shapes=[pltpu.SemaphoreType.DMA((2,)), pltpu.SemaphoreType.DMA((2,))],
        compiler_params=pltpu.CompilerParams(collective_id=0, has_side_effects=True),
        name="halo",
    )(x)


def iota(shape, dim):
    return lax.broadcasted_iota(I32, shape, dim)


def one_hot(mask):
    return jnp.where(mask, 1.0, 0.0).astype(BF16)


def unpack(src_ref, plain, k):
    for t in range(DATES):
        for r in range(STRIP):
            pair = src_ref[t, r].astype(F32)
            row = (t * STRIP + r) * 2
            plain[k, 0, pl.ds(row, 2)] = pair[:, :128]
            plain[k, 1, pl.ds(row, 2)] = pair[:, 128:]


def spread(plain, k, r, row, x_ref, keep):
    for h in range(2):
        for comp in range(2):
            v = plain[k, h, pl.ds(r * 2 + comp, DATES, stride=STRIP * 2)]
            if keep is not None:
                v = jnp.where(keep, v, 0.0)
            x_ref[comp, h, pl.ds(row * XS, DATES)] = v
            x_ref[comp, h, pl.ds(row * XS + DATES, 8)] = v[:8]


def row_sums(terms):
    total = terms(10)
    for row in range(9, 4, -1):
        total = total + terms(row)
    sums = [None] * STRIP
    sums[5] = total
    for row in range(4, -1, -1):
        total = total + terms(row)
        sums[row] = total
    tail = None
    for r in range(1, STRIP):
        term = terms(r + 10)
        tail = term if tail is None else tail + term
        sums[r] = sums[r] + tail
    return sums


def pair_sums(terms):
    a, b = [], []

    def add(x, y):
        return (x[0] + y[0], x[1] + y[1])

    total = terms(10)
    for row in range(9, 4, -1):
        total = add(total, terms(row))
    sums = [None] * STRIP
    sums[5] = total
    for row in range(4, -1, -1):
        total = add(total, terms(row))
        sums[row] = total
    tail = None
    for r in range(1, STRIP):
        term = terms(r + 10)
        tail = term if tail is None else add(tail, term)
        sums[r] = add(sums[r], tail)
    return sums


def split_store(ref, lead, row, h, value):
    high = value.astype(BF16)
    low = (value - high.astype(F32)).astype(BF16)
    ref[lead, pl.ds(row, 16), h * 128 : (h + 1) * 128] = high
    ref[lead, pl.ds(row, 16), 256 + h * 128 : 256 + (h + 1) * 128] = low


def coherences(x_ref, sums_ref, band_ref, scale_ref, g_ref):
    band_ref[...] = one_hot(
        jnp.abs((iota((512, 256), 0) & 255) - iota((512, 256), 1)) <= 2
    )
    for h in range(2):

        def power(row):
            re = x_ref[0, h, pl.ds(row * XS, 16)]
            im = x_ref[1, h, pl.ds(row * XS, 16)]
            return re * re + im * im

        for r, value in enumerate(row_sums(power)):
            split_store(sums_ref, 0, r * 16, h, value)
    energy = jnp.dot(sums_ref[0, :96], band_ref[...], preferred_element_type=F32) + 1.0
    scale = lax.rsqrt(energy)
    for h in range(2):
        for r in range(STRIP):
            v = scale[r * 16 : (r + 1) * 16, h * 128 : (h + 1) * 128]
            scale_ref[h, pl.ds(r * XS, 16)] = v
            scale_ref[h, pl.ds(r * XS + DATES, 8)] = v[:8]
    for d in range(1, 8):
        for h in range(2):

            def product(row):
                are = x_ref[0, h, pl.ds(row * XS, 16)]
                aim = x_ref[1, h, pl.ds(row * XS, 16)]
                bre = x_ref[0, h, pl.ds(row * XS + d, 16)]
                bim = x_ref[1, h, pl.ds(row * XS + d, 16)]
                return (are * bre + aim * bim, aim * bre - are * bim)

            for r, pair in enumerate(pair_sums(product)):
                for part in range(2):
                    split_store(sums_ref, d, r * 32 + part * 16, h, pair[part])
        summed = jnp.dot(sums_ref[d], band_ref[...], preferred_element_type=F32)
        for h in range(2):
            for r in range(STRIP):
                both = scale_ref[h, pl.ds(r * XS, 16)] * scale_ref[h, pl.ds(r * XS + d, 16)]
                for part in range(2):
                    row = r * 32 + part * 16
                    v = summed[row : row + 16, h * 128 : (h + 1) * 128] * both
                    v = v.astype(BF16).astype(F32)
                    base = ((d - 1) * 2 + part) * 128
                    g_ref[h, pl.ds(base + r, 16, stride=8)] = v


def power_iterations(g_ref, plain, v_ref, c_ref, here):
    def entry(h, a, b):
        d = (b - a) % DATES
        flip = d > 7
        if flip:
            a, d = b, DATES - d
        base = (d - 1) * 256 + a * 8
        re = g_ref[h, pl.ds(base, STRIP)]
        im = g_ref[h, pl.ds(base + 128, STRIP)]
        return re, im, flip

    def normalized(parts):
        energy = None
        for re, im in parts:
            term = re * re + im * im
            energy = term if energy is None else energy + term
        factor = lax.rsqrt(energy * (1.0 / DATES) + 0.25)
        return tuple((re * factor, im * factor) for re, im in parts)

    def half(h, _):
        first = []
        for a in range(DATES):
            re, im = jnp.ones((STRIP, 128), F32), jnp.zeros((STRIP, 128), F32)
            for b in range(DATES):
                if b != a:
                    gre, gim, flip = entry(h, a, b)
                    re = re + gre
                    im = im - gim if flip else im + gim
            first.append((re, im))
        vec = normalized(first)

        def step(_, vec):
            out = []
            for a in range(DATES):
                re, im = vec[a]
                for b in range(DATES):
                    if b != a:
                        gre, gim, flip = entry(h, a, b)
                        vre, vim = vec[b]
                        if flip:
                            re = re + (gre * vre + gim * vim)
                            im = im + (gre * vim - gim * vre)
                        else:
                            re = re + (gre * vre - gim * vim)
                            im = im + (gre * vim + gim * vre)
                out.append((re, im))
            return normalized(out)

        vec = lax.fori_loop(0, ITERS - 1, step, vec)
        packed_re, packed_im = None, None
        for t in range(DATES):
            vre, vim = vec[t]
            sre = plain[0, h, pl.ds(t * STRIP * 2, STRIP, stride=2)]
            sim = plain[0, h, pl.ds(t * STRIP * 2 + 1, STRIP, stride=2)]
            re = vre * sre + vim * sim
            im = vre * sim - vim * sre
            packed_re = re if packed_re is None else packed_re + re
            packed_im = im if packed_im is None else packed_im + im
            v_ref[h, pl.ds(t * 8, STRIP)] = vre
            v_ref[h, pl.ds((16 + t) * 8, STRIP)] = vim
        norm = 1.0 / math.sqrt(DATES)
        packed_re, packed_im = packed_re * norm, packed_im * norm
        v_ref[h, pl.ds(15 * 8, STRIP)] = packed_re
        v_ref[h, pl.ds(31 * 8, STRIP)] = packed_im
        c_ref[here, 0, h] = packed_re
        c_ref[here, 1, h] = packed_im
        return 0

    lax.fori_loop(0, 2, half, 0)


def connect(v_ref, c_ref, here):
    for h in range(2):
        datum_re, datum_im = jnp.ones((STRIP, 128), F32), jnp.zeros((STRIP, 128), F32)
        for j in range(SECT - 1):
            ere, eim = c_ref[j, 0, h], c_ref[j, 1, h]
            lre, lim = c_ref[j + 1, 0, h], c_ref[j + 1, 1, h]
            link_re = lre * ere + lim * eim
            link_im = lim * ere - lre * eim
            factor = lax.rsqrt(link_re * link_re + link_im * link_im + 1.0)
            ure, uim = link_re * factor, link_im * factor
            new_re = datum_re * ure - datum_im * uim
            new_im = datum_re * uim + datum_im * ure
            reached = j < here
            datum_re = jnp.where(reached, new_re, datum_re)
            datum_im = jnp.where(reached, new_im, datum_im)
        for t in range(DATES):
            vre = v_ref[h, pl.ds(t * 8, STRIP)]
            vim = v_ref[h, pl.ds((16 + t) * 8, STRIP)]
            v_ref[h, pl.ds(t * 8, STRIP)] = vre * datum_re - vim * datum_im
            v_ref[h, pl.ds((16 + t) * 8, STRIP)] = vre * datum_im + vim * datum_re


def main_kernel(
    x_ref,
    halo_ref,
    map_ref,
    linked_ref,
    compressed_ref,
    plain,
    x2_ref,
    sums_ref,
    band_ref,
    scale_ref,
    g_ref,
    v_ref,
    c_ref,
    pick_ref,
    rows_ref,
    rows2_ref,
    send1,
    recv1,
    send2,
    recv2,
    spread_ref,
    sem_cs,
    sem_cr,
    sem_1s,
    sem_1r,
    sem_2s,
    sem_2r,
):
    section = lax.axis_index("stack")
    me = lax.axis_index("pix")
    y, rest = me // (NZ * NC), lax.rem(me, NZ * NC)
    z, c = rest // NC, lax.rem(rest, NC)
    g = y * NC + c

    sections = [lax.rem(section + o, SECT) for o in range(1, SECT)]
    group_of = [lax.rem(g + o, GROUPS) for o in range(1, GROUPS)]
    groups = [place(q // NC, z, lax.rem(q, NC)) for q in group_of]
    z_of = [lax.rem(z + o, NZ) for o in range(1, NZ)]
    depths = [place(y, q, c) for q in z_of]

    barrier = pltpu.get_barrier_semaphore()
    for peer in sections:
        pl.semaphore_signal(barrier, inc=1, device_id={"stack": peer}, device_id_type=MESH)
    for peer in groups + depths:
        pl.semaphore_signal(barrier, inc=1, device_id={"pix": peer}, device_id_type=MESH)

    m = iota((128, 128), 0)
    slot = (m >> 5) * 32 + (m & 15) * 2 + ((m >> 4) & 1)
    owner = jnp.broadcast_to(map_ref[...], (128, 128))
    chosen = one_hot(slot == owner)
    column = iota((128, 256), 1)
    block = iota((128, 256), 0)
    for k in range(2):
        pick = jnp.dot(chosen, one_hot(column == 2 * block + k), preferred_element_type=F32)
        pick_ref[:, k * 256 : (k + 1) * 256] = pick.astype(BF16)

    unpack(x_ref, plain, 0)
    unpack(halo_ref.at[0], plain, 1)
    unpack(halo_ref.at[1], plain, 2)
    for r in range(STRIP):
        spread(plain, 0, r, UP + r, x2_ref, None)
    for r in range(1, STRIP):
        spread(plain, 1, r, r - 1, x2_ref, me > 0)
    for r in range(UP):
        spread(plain, 2, r, UP + STRIP + r, x2_ref, me < BLOCKS - 1)
    coherences(x2_ref, sums_ref, band_ref, scale_ref, g_ref)
    power_iterations(g_ref, plain, v_ref, c_ref, section)

    pl.semaphore_wait(barrier, len(sections) + len(groups) + len(depths))

    sends = []

    def send(src, dst, ssem, rsem, device):
        copy = pltpu.make_async_remote_copy(
            src_ref=src, dst_ref=dst, send_sem=ssem, recv_sem=rsem,
            device_id=device, device_id_type=MESH,
        )
        copy.start()
        sends.append(copy)
        return copy

    first = [
        send(c_ref.at[section], c_ref.at[section], sem_cs.at[o], sem_cr.at[o], {"stack": peer})
        for o, peer in enumerate(sections)
    ]
    for copy in first:
        copy.wait_recv()
    connect(v_ref, c_ref, section)

    for h in range(2):
        lanes = slice(h * 128, (h + 1) * 128)
        for r in range(4):
            v = v_ref[h, pl.ds(r, FEAT, stride=8)].astype(BF16)
            rows_ref[r * FEAT : (r + 1) * FEAT, lanes] = v
        for r in range(2):
            v = v_ref[h, pl.ds(4 + r, FEAT, stride=8)].astype(BF16)
            for k in range(2):
                at = (k * 2 + r) * FEAT
                rows2_ref[at : at + FEAT, k * 256 + h * 128 : k * 256 + (h + 1) * 128] = v
                rows2_ref[at : at + FEAT, (1 - k) * 256 + h * 128 : (1 - k) * 256 + (h + 1) * 128] = (
                    jnp.zeros((FEAT, 128), BF16)
                )
    for k in range(2):
        part = lax.dot_general(
            pick_ref[:, k * 256 : (k + 1) * 256], rows_ref[...], NT_DIMS, preferred_element_type=F32
        ).astype(BF16)
        for q in range(GROUPS):
            send1[q, :, k * 128 : (k + 1) * 128] = part[q * 16 : (q + 1) * 16]
    part = lax.dot_general(
        pick_ref[...], rows2_ref[...], NT_DIMS, preferred_element_type=F32
    ).astype(BF16)
    for q in range(GROUPS):
        send1[q, :, 256:384] = part[q * 16 : (q + 1) * 16]

    second = [
        send(send1.at[q], recv1.at[g], sem_1s.at[o], sem_1r.at[o], {"pix": peer})
        for o, (q, peer) in enumerate(zip(group_of, groups))
    ]
    recv1[g] = send1[g]
    i, j = iota((128, 128), 0), iota((128, 128), 1)
    turn = one_hot(j == (i & 7) * 16 + (i >> 3))
    for copy in second:
        copy.wait_recv()
    got = recv1[...].reshape(128, 384)
    moved = jnp.dot(turn, got, preferred_element_type=F32)
    for q in range(NZ):
        send2[q] = moved[q * 8 : (q + 1) * 8].astype(BF16)
    order = sorted(range(NZ - 1), key=lambda o: -min(o + 1, NZ - 1 - o))
    third = [
        send(send2.at[z_of[o]], recv2.at[z], sem_2s.at[o], sem_2r.at[o], {"pix": depths[o]})
        for o in order
    ]
    recv2[z] = send2[z]
    n, lane = iota((128, ROWS), 0), iota((128, ROWS), 1)
    strip = ((n >> 1) & 3) * 32 + (n >> 3) * 2 + (n & 1)
    for r in range(STRIP):
        spread_ref[r * 128 : (r + 1) * 128] = one_hot(lane == strip * STRIP + r)
    for copy in third:
        copy.wait_recv()
    got = jnp.concatenate([recv2[q].astype(F32) for q in range(NZ)], axis=0)
    turned = got.T.astype(BF16)
    blocks = []
    for k in range(2):
        pieces = []
        for r in range(STRIP):
            at = k * 128 + r * FEAT if r < 4 else 256 + (k * 2 + r - 4) * FEAT
            pieces.append(turned[at : at + FEAT])
        blocks.append(jnp.concatenate(pieces, axis=1))
    out = jnp.dot(jnp.concatenate(blocks, axis=0), spread_ref[...], preferred_element_type=F32)
    for k in range(2):
        lanes = slice(k * ROWS, (k + 1) * ROWS)
        for part in range(2):
            at = k * FEAT + part * 16
            linked_ref[part, :, lanes] = out[at : at + DATES]
            compressed_ref[part : part + 1, lanes] = out[at + DATES : at + DATES + 1]
    for copy in sends:
        copy.wait_send()


def run_main(x, halo, owner_map):
    vmem = pl.BlockSpec(memory_space=pltpu.VMEM)
    return pl.pallas_call(
        main_kernel,
        out_shape=(
            jax.ShapeDtypeStruct((2, DATES, 2 * ROWS), F32),
            jax.ShapeDtypeStruct((2, 2 * ROWS), F32),
        ),
        in_specs=[vmem] * 3,
        out_specs=(vmem, vmem),
        scratch_shapes=[
            pltpu.VMEM((3, 2, DATES * STRIP * 2, 128), F32),
            pltpu.VMEM((2, 2, TALL * XS, 128), F32),
            pltpu.VMEM((8, STRIP * 32, 512), BF16),
            pltpu.VMEM((512, 256), BF16),
            pltpu.VMEM((2, STRIP * XS, 128), F32),
            pltpu.VMEM((2, 7 * 2 * 128, 128), F32),
            pltpu.VMEM((2, FEAT * 8, 128), F32),
            pltpu.VMEM((SECT, 2, 2, STRIP, 128), F32),
            pltpu.VMEM((128, 512), BF16),
            pltpu.VMEM((128, 256), BF16),
            pltpu.VMEM((128, 512), BF16),
            pltpu.VMEM((GROUPS, NZ, 384), BF16),
            pltpu.VMEM((GROUPS, NZ, 384), BF16),
            pltpu.VMEM((NZ, GROUPS, 384), BF16),
            pltpu.VMEM((NZ, GROUPS, 384), BF16),
            pltpu.VMEM((ROWS, ROWS), BF16),
            pltpu.SemaphoreType.DMA((SECT - 1,)),
            pltpu.SemaphoreType.DMA((SECT - 1,)),
            pltpu.SemaphoreType.DMA((GROUPS - 1,)),
            pltpu.SemaphoreType.DMA((GROUPS - 1,)),
            pltpu.SemaphoreType.DMA((NZ - 1,)),
            pltpu.SemaphoreType.DMA((NZ - 1,)),
        ],
        compiler_params=pltpu.CompilerParams(collective_id=1, has_side_effects=True),
        name="link",
    )(x, halo, owner_map)


def local(slc, owner_map):
    x = jnp.transpose(slc[:, 0], (1, 2, 0, 3))
    halo = exchange_halo(x)
    linked, compressed = run_main(x, halo, owner_map.reshape(1, BLOCKS))
    return (
        linked.reshape(2, 1, DATES, 1, 2 * ROWS),
        compressed.reshape(2, 1, 1, 2 * ROWS),
    )


def solution(mesh):
    in_specs = (P(None, "stack", None, "pix", None), P())
    out_specs = (P(None, "stack", None, "pix", None), P(None, "stack", "pix", None))
    return jax.shard_map(local, mesh=mesh, in_specs=in_specs, out_specs=out_specs, check_vma=False)
```

```python
import math

import jax
import jax.numpy as jnp
from jax import lax
from jax.experimental import pallas as pl
from jax.experimental.pallas import tpu as pltpu
from jax.sharding import PartitionSpec as P

MESH = pl.DeviceIdType.MESH
F32, BF16, I32 = jnp.float32, jnp.bfloat16, jnp.int32
DATES, ITERS, SECT, ROWS, COLS, BLOCKS = 15, 8, 4, 768, 256, 128
STRIP = 6
UP = 5
TALL = 16
NY, NZ, NC = 4, 16, 2
GROUPS = NY * NC
FEAT = 32
XS = 24
NT_DIMS = (((1,), (1,)), ((), ()))


def place(y, z, c):
    return y * (NZ * NC) + z * NC + c


def iota(shape, dim):
    return lax.broadcasted_iota(I32, shape, dim)


def one_hot(mask):
    return jnp.where(mask, 1.0, 0.0).astype(BF16)


def unpack(src_ref, plain, k, rows):
    for t in range(DATES):
        for r in range(rows):
            pair = src_ref[t, r].astype(F32)
            row = (t * STRIP + r) * 2
            plain[k, 0, pl.ds(row, 2)] = pair[:, :128]
            plain[k, 1, pl.ds(row, 2)] = pair[:, 128:]


def spread(plain, k, r, row, x_ref, keep):
    for h in range(2):
        for comp in range(2):
            v = plain[k, h, pl.ds(r * 2 + comp, DATES, stride=STRIP * 2)]
            if keep is not None:
                v = jnp.where(keep, v, 0.0)
            x_ref[comp, h, pl.ds(row * XS, DATES)] = v
            x_ref[comp, h, pl.ds(row * XS + DATES, 8)] = v[:8]


def add(x, y):
    return tuple(p + q for p, q in zip(x, y))


def middle_sum(terms):
    total = terms(UP)
    for row in range(UP + 1, UP + STRIP):
        total = add(total, terms(row))
    return total


def window_sums(terms, middle):
    total = middle
    sums = [None] * STRIP
    sums[5] = total
    for row in range(4, -1, -1):
        total = add(total, terms(row))
        sums[row] = total
    tail = None
    for r in range(1, STRIP):
        term = terms(r + 10)
        tail = term if tail is None else add(tail, term)
        sums[r] = add(sums[r], tail)
    return sums


def split_store(ref, lead, row, h, value):
    high = value.astype(BF16)
    low = (value - high.astype(F32)).astype(BF16)
    ref[lead, pl.ds(row, 16), h * 128 : (h + 1) * 128] = high
    ref[lead, pl.ds(row, 16), 256 + h * 128 : 256 + (h + 1) * 128] = low


def products(x_ref, h, d):
    def power(row):
        re = x_ref[0, h, pl.ds(row * XS, 16)]
        im = x_ref[1, h, pl.ds(row * XS, 16)]
        return (re * re + im * im,)

    def product(row):
        are = x_ref[0, h, pl.ds(row * XS, 16)]
        aim = x_ref[1, h, pl.ds(row * XS, 16)]
        bre = x_ref[0, h, pl.ds(row * XS + d, 16)]
        bim = x_ref[1, h, pl.ds(row * XS + d, 16)]
        return (are * bre + aim * bim, aim * bre - are * bim)

    return product if d else power


def middles(x_ref, mid_ref):
    for d in range(8):
        for h in range(2):
            for part, value in enumerate(middle_sum(products(x_ref, h, d))):
                mid_ref[d, h, part] = value


def coherences(x_ref, mid_ref, sums_ref, band_ref, scale_ref, g_ref):
    for d in range(8):
        parts = 2 if d else 1
        for h in range(2):
            middle = tuple(mid_ref[d, h, part] for part in range(parts))
            for r, value in enumerate(window_sums(products(x_ref, h, d), middle)):
                for part in range(parts):
                    split_store(sums_ref, d, (r * parts + part) * 16, h, value[part])
        rows = STRIP * parts * 16
        summed = jnp.dot(sums_ref[d, :rows], band_ref[...], preferred_element_type=F32)
        if not d:
            scale = lax.rsqrt(summed + 1.0)
            for h in range(2):
                for r in range(STRIP):
                    v = scale[r * 16 : (r + 1) * 16, h * 128 : (h + 1) * 128]
                    scale_ref[h, pl.ds(r * XS, 16)] = v
                    scale_ref[h, pl.ds(r * XS + DATES, 8)] = v[:8]
            continue
        for h in range(2):
            for r in range(STRIP):
                both = scale_ref[h, pl.ds(r * XS, 16)] * scale_ref[h, pl.ds(r * XS + d, 16)]
                row = r * 32
                re = summed[row : row + 16, h * 128 : (h + 1) * 128] * both
                im = summed[row + 16 : row + 32, h * 128 : (h + 1) * 128] * both
                re, im = re.astype(BF16).astype(F32), im.astype(BF16).astype(F32)
                base = (d - 1) * 384 + r
                g_ref[h, pl.ds(base, 16, stride=8)] = re
                g_ref[h, pl.ds(base + 128, 16, stride=8)] = re + im
                g_ref[h, pl.ds(base + 256, 16, stride=8)] = im - re


def power_iterations(g_ref, plain, v_ref, c_ref):
    def at(a, b):
        d = (b - a) % DATES
        flip = d > 7
        if flip:
            a, d = b, DATES - d
        return (d - 1) * 384 + a * 8, flip

    def normalized(parts):
        energy = None
        for re, im in parts:
            term = re * re + im * im
            energy = term if energy is None else energy + term
        factor = lax.rsqrt(energy * (1.0 / DATES) + 0.25)
        return tuple((re * factor, im * factor) for re, im in parts)

    def half(h, _):
        first = []
        for a in range(DATES):
            re, im = jnp.ones((STRIP, 128), F32), jnp.zeros((STRIP, 128), F32)
            for b in range(DATES):
                if b != a:
                    base, flip = at(a, b)
                    gre = g_ref[h, pl.ds(base, STRIP)]
                    gim = g_ref[h, pl.ds(base + 128, STRIP)] - gre
                    re = re + gre
                    im = im - gim if flip else im + gim
            first.append((re, im))
        vec = normalized(first)

        def step(_, vec):
            both = [re + im for re, im in vec]
            out = []
            for a in range(DATES):
                one, two, three = None, None, None
                for b in range(DATES):
                    if b != a:
                        base, flip = at(a, b)
                        vre, vim = vec[b]
                        gre = g_ref[h, pl.ds(base, STRIP)]
                        plus = g_ref[h, pl.ds(base + 128, STRIP)]
                        minus = g_ref[h, pl.ds(base + 256, STRIP)]
                        p1 = gre * both[b]
                        one = p1 if one is None else one + p1
                        p2, p3 = (plus * vre, minus * vim) if flip else (minus * vre, plus * vim)
                        if two is None:
                            two, three = (-p2, -p3) if flip else (p2, p3)
                        elif flip:
                            two, three = two - p2, three - p3
                        else:
                            two, three = two + p2, three + p3
                out.append((vec[a][0] + (one - three), vec[a][1] + (one + two)))
            return normalized(out)

        vec = lax.fori_loop(0, ITERS - 1, step, vec)
        packed_re, packed_im = None, None
        for t in range(DATES):
            vre, vim = vec[t]
            sre = plain[0, h, pl.ds(t * STRIP * 2, STRIP, stride=2)]
            sim = plain[0, h, pl.ds(t * STRIP * 2 + 1, STRIP, stride=2)]
            re = vre * sre + vim * sim
            im = vre * sim - vim * sre
            packed_re = re if packed_re is None else packed_re + re
            packed_im = im if packed_im is None else packed_im + im
            v_ref[h, pl.ds(t * 8, STRIP)] = vre
            v_ref[h, pl.ds((16 + t) * 8, STRIP)] = vim
        norm = 1.0 / math.sqrt(DATES)
        c_ref[0, h] = packed_re * norm
        c_ref[1, h] = packed_im * norm
        return 0

    lax.fori_loop(0, 2, half, 0)


def main_kernel(
    x_hbm,
    map_hbm,
    out_ref,
    map_ref,
    x_ref,
    halo_ref,
    plain,
    x2_ref,
    mid_ref,
    sums_ref,
    band_ref,
    scale_ref,
    g_ref,
    v_ref,
    c_ref,
    pick_ref,
    rows_ref,
    rows2_ref,
    rows3_ref,
    send1,
    recv1,
    sendc,
    recvc,
    send2,
    recv2,
    sem_x,
    sem_hs,
    sem_hr,
    sem_cs,
    sem_cr,
    sem_1s,
    sem_1r,
    sem_2s,
    sem_2r,
):
    section = lax.axis_index("stack")
    me = lax.axis_index("pix")
    y, rest = me // (NZ * NC), lax.rem(me, NZ * NC)
    z, c = rest // NC, lax.rem(rest, NC)
    g = y * NC + c

    sections = [lax.rem(section + o, SECT) for o in range(SECT)]
    group_of = [lax.rem(g + o, GROUPS) for o in range(GROUPS)]
    groups = [place(q // NC, z, lax.rem(q, NC)) for q in group_of]
    plane = [(s, o) for s in range(SECT) for o in range(GROUPS) if s or o]
    plane.sort(key=lambda so: -(min(so[0], 4 - so[0]) + min(so[1] // 2, 4 - so[1] // 2)))
    z_of = [lax.rem(z + o, NZ) for o in range(1, NZ)]
    depths = [place(y, q, c) for q in z_of]
    after, before = lax.rem(me + 1, BLOCKS), lax.rem(me + BLOCKS - 1, BLOCKS)
    other = lax.rem(me + BLOCKS + 2 * c - 1, BLOCKS)

    def device(s, o):
        return {"stack": sections[s], "pix": groups[o]}

    barrier = pltpu.get_barrier_semaphore()
    pl.semaphore_signal(barrier, inc=1, device_id={"pix": other}, device_id_type=MESH)
    for s, o in reversed(plane):
        pl.semaphore_signal(barrier, inc=1, device_id=device(s, o), device_id_type=MESH)
    for peer in depths:
        pl.semaphore_signal(barrier, inc=1, device_id={"pix": peer}, device_id_type=MESH)
    slots = pltpu.make_async_copy(map_hbm, map_ref, sem_x.at[0])
    slots.start()
    own = pltpu.make_async_copy(x_hbm, x_ref, sem_x.at[1])
    own.start()
    pl.semaphore_wait(barrier, 1 + len(plane) + len(depths))

    sends = []

    def send(src, dst, ssem, rsem, device):
        copy = pltpu.make_async_remote_copy(
            src_ref=src, dst_ref=dst, send_sem=ssem, recv_sem=rsem,
            device_id=device, device_id_type=MESH,
        )
        copy.start()
        sends.append(copy)
        return copy

    halos = [
        send(x_hbm.at[:, 1:6], halo_ref.at[0], sem_hs.at[0], sem_hr.at[0], {"pix": after}),
        send(x_hbm.at[:, 0:5], halo_ref.at[1], sem_hs.at[1], sem_hr.at[1], {"pix": before}),
    ]

    m = iota((128, 128), 0)
    slot = (m >> 5) * 32 + (m & 15) * 2 + ((m >> 4) & 1)
    slots.wait()
    owner = jnp.broadcast_to(map_ref[...], (128, 128))
    chosen = one_hot(slot == owner)
    column = iota((128, 256), 1)
    block = iota((128, 256), 0)
    for k in range(2):
        pick = jnp.dot(chosen, one_hot(column == 2 * block + k), preferred_element_type=F32)
        pick_ref[:, k * 256 : (k + 1) * 256] = pick.astype(BF16)
    band_ref[...] = one_hot(
        jnp.abs((iota((512, 256), 0) & 255) - iota((512, 256), 1)) <= 2
    )
    rows3_ref[...] = jnp.zeros((128, 512), F32)
    for h in range(2):
        for part in range(2):
            v_ref[h, pl.ds((part * 16 + DATES) * 8, 8)] = jnp.zeros((8, 128), F32)

    own.wait()
    unpack(x_ref, plain, 0, STRIP)
    for r in range(STRIP):
        spread(plain, 0, r, UP + r, x2_ref, None)
    middles(x2_ref, mid_ref)
    for copy in halos:
        copy.wait_recv()
    unpack(halo_ref.at[0], plain, 1, UP)
    unpack(halo_ref.at[1], plain, 2, UP)
    for r in range(UP):
        spread(plain, 1, r, r, x2_ref, me > 0)
        spread(plain, 2, r, UP + STRIP + r, x2_ref, me < BLOCKS - 1)
    coherences(x2_ref, mid_ref, sums_ref, band_ref, scale_ref, g_ref)
    power_iterations(g_ref, plain, v_ref, c_ref)

    for h in range(2):
        for comp in range(2):
            for k in range(2):
                at = pl.multiple_of(comp * 64 + k * 32 + section * 8, 8)
                lanes = slice(k * 256 + h * 128, k * 256 + (h + 1) * 128)
                rows3_ref[pl.ds(at, STRIP), lanes] = c_ref[comp, h]
    part = lax.dot_general(
        pick_ref[...], rows3_ref[...].astype(BF16), NT_DIMS, preferred_element_type=F32
    ).astype(BF16)
    for q in range(GROUPS):
        sendc[q] = part[q * 16 : (q + 1) * 16]
    first = [
        send(sendc.at[group_of[o]], recvc.at[section, g], sem_cs.at[s, o], sem_cr.at[s, o], device(s, o))
        for s, o in plane
    ]

    for h in range(2):
        lanes = slice(h * 128, (h + 1) * 128)
        for r in range(4):
            v = v_ref[h, pl.ds(r, FEAT, stride=8)].astype(BF16)
            rows_ref[r * FEAT : (r + 1) * FEAT, lanes] = v
        for r in range(2):
            v = v_ref[h, pl.ds(4 + r, FEAT, stride=8)].astype(BF16)
            for k in range(2):
                at = (k * 2 + r) * FEAT
                rows2_ref[at : at + FEAT, k * 256 + h * 128 : k * 256 + (h + 1) * 128] = v
                rows2_ref[at : at + FEAT, (1 - k) * 256 + h * 128 : (1 - k) * 256 + (h + 1) * 128] = (
                    jnp.zeros((FEAT, 128), BF16)
                )
    for k in range(2):
        part = lax.dot_general(
            pick_ref[:, k * 256 : (k + 1) * 256], rows_ref[...], NT_DIMS, preferred_element_type=F32
        ).astype(BF16)
        for q in range(GROUPS):
            send1[q, :, k * 128 : (k + 1) * 128] = part[q * 16 : (q + 1) * 16]
    part = lax.dot_general(
        pick_ref[...], rows2_ref[...], NT_DIMS, preferred_element_type=F32
    ).astype(BF16)
    for q in range(GROUPS):
        send1[q, :, 256:384] = part[q * 16 : (q + 1) * 16]
    second = [
        send(send1.at[group_of[o]], recv1.at[g], sem_1s.at[o], sem_1r.at[o], device(0, o))
        for s, o in plane
        if s == 0
    ]
    recvc[section, g] = sendc[g]
    recv1[g] = send1[g]
    i, j = iota((128, 128), 0), iota((128, 128), 1)
    turn = one_hot(j == (i & 7) * 16 + (i >> 3))
    for copy in first + second:
        copy.wait_recv()
    got = recv1[...].reshape(128, 384)
    moved = jnp.dot(turn, got, preferred_element_type=F32)
    for q in range(NZ):
        send2[q, :, :384] = moved[q * 8 : (q + 1) * 8].astype(BF16)
    packed = (recvc[0] + recvc[1] + recvc[2] + recvc[3]).reshape(128, 128)
    moved = jnp.dot(turn, packed, preferred_element_type=F32)
    for q in range(NZ):
        send2[q, :, 384:] = moved[q * 8 : (q + 1) * 8].astype(BF16)
    order = sorted(range(NZ - 1), key=lambda o: -min(o + 1, NZ - 1 - o))
    third = [
        send(send2.at[z_of[o]], recv2.at[z], sem_2s.at[o], sem_2r.at[o], {"pix": depths[o]})
        for o in order
    ]
    recv2[z] = send2[z]
    for copy in third:
        copy.wait_recv()
    out_ref[...] = recv2[...]
    for copy in sends:
        copy.wait_send()


def run_main(x, owner_map):
    vmem = pl.BlockSpec(memory_space=pltpu.VMEM)
    dma = pltpu.SemaphoreType.DMA
    return pl.pallas_call(
        main_kernel,
        out_shape=jax.ShapeDtypeStruct((NZ, GROUPS, 512), BF16),
        in_specs=[pl.BlockSpec(memory_space=pltpu.HBM)] * 2,
        out_specs=vmem,
        scratch_shapes=[
            pltpu.VMEM((1, BLOCKS), I32),
            pltpu.VMEM((DATES, STRIP, 2, COLS), BF16),
            pltpu.VMEM((2, DATES, UP, 2, COLS), BF16),
            pltpu.VMEM((3, 2, DATES * STRIP * 2, 128), F32),
            pltpu.VMEM((2, 2, TALL * XS, 128), F32),
            pltpu.VMEM((8, 2, 2, 16, 128), F32),
            pltpu.VMEM((8, STRIP * 32, 512), BF16),
            pltpu.VMEM((512, 256), BF16),
            pltpu.VMEM((2, STRIP * XS, 128), F32),
            pltpu.VMEM((2, 7 * 3 * 128, 128), F32),
            pltpu.VMEM((2, FEAT * 8, 128), F32),
            pltpu.VMEM((2, 2, STRIP, 128), F32),
            pltpu.VMEM((128, 512), BF16),
            pltpu.VMEM((128, 256), BF16),
            pltpu.VMEM((128, 512), BF16),
            pltpu.VMEM((128, 512), F32),
            pltpu.VMEM((GROUPS, NZ, 384), BF16),
            pltpu.VMEM((GROUPS, NZ, 384), BF16),
            pltpu.VMEM((GROUPS, NZ, 128), BF16),
            pltpu.VMEM((SECT, GROUPS, NZ, 128), BF16),
            pltpu.VMEM((NZ, GROUPS, 512), BF16),
            pltpu.VMEM((NZ, GROUPS, 512), BF16),
            dma((2,)),
            dma((2,)),
            dma((2,)),
            dma((SECT, GROUPS)),
            dma((SECT, GROUPS)),
            dma((GROUPS,)),
            dma((GROUPS,)),
            dma((NZ - 1,)),
            dma((NZ - 1,)),
        ],
        compiler_params=pltpu.CompilerParams(
            collective_id=0, has_side_effects=True, vmem_limit_bytes=20 * 1024 * 1024
        ),
        name="link",
    )(x, owner_map)


def finish_kernel(got_ref, linked_ref, compressed_ref, turned_ref, spread_ref):
    section = lax.axis_index("stack")
    n, lane = iota((128, ROWS), 0), iota((128, ROWS), 1)
    strip = ((n >> 1) & 3) * 32 + (n >> 3) * 2 + (n & 1)
    for r in range(STRIP):
        spread_ref[r * 128 : (r + 1) * 128] = one_hot(lane == strip * STRIP + r)
    got = jnp.concatenate([got_ref[q].astype(F32) for q in range(NZ)], axis=0)
    for tile in range(4):
        turned_ref[tile * 128 : (tile + 1) * 128] = got[:, tile * 128 : (tile + 1) * 128].T
    blocks = []
    for k in range(2):
        pieces = []
        for r in range(STRIP):
            at = k * 128 + r * FEAT if r < 4 else 256 + (k * 2 + r - 4) * FEAT
            pieces.append(turned_ref[pl.ds(at, FEAT)].astype(BF16))
        blocks.append(jnp.concatenate(pieces, axis=1))
    pieces = []
    for r in range(STRIP):
        pair = [turned_ref[pl.ds(384 + comp * 64 + r, 8, stride=8)] for comp in range(2)]
        pieces.append(jnp.concatenate(pair, axis=0).astype(BF16))
    blocks.append(jnp.concatenate(pieces, axis=1))
    out = jnp.dot(jnp.concatenate(blocks, axis=0), spread_ref[...], preferred_element_type=F32)
    re, im = out[64:72], out[72:80]
    link_re = re[1:] * re[:-1] + im[1:] * im[:-1]
    link_im = im[1:] * re[:-1] - re[1:] * im[:-1]
    factor = lax.rsqrt(link_re * link_re + link_im * link_im + 1.0)
    unit_re, unit_im = link_re * factor, link_im * factor
    tiles = ROWS // 128
    for k in range(2):
        datum_re, datum_im = jnp.ones((1, ROWS), F32), jnp.zeros((1, ROWS), F32)
        mine_re, mine_im = re[k * 4 : k * 4 + 1], im[k * 4 : k * 4 + 1]
        for j in range(SECT - 1):
            at = k * 4 + j
            ure, uim = unit_re[at : at + 1], unit_im[at : at + 1]
            new_re = datum_re * ure - datum_im * uim
            new_im = datum_re * uim + datum_im * ure
            reached = j < section
            datum_re = jnp.where(reached, new_re, datum_re)
            datum_im = jnp.where(reached, new_im, datum_im)
            mine_re = jnp.where(reached, re[at + 1 : at + 2], mine_re)
            mine_im = jnp.where(reached, im[at + 1 : at + 2], mine_im)
        at = k * FEAT
        vre, vim = out[at : at + DATES], out[at + 16 : at + 16 + DATES]
        linked = (vre * datum_re - vim * datum_im, vre * datum_im + vim * datum_re)
        mine = (mine_re, mine_im)
        for part in range(2):
            for tile in range(tiles):
                row = part * DATES * 2 * tiles + k * tiles + tile
                lanes = slice(tile * 128, (tile + 1) * 128)
                linked_ref[pl.ds(row, DATES, stride=2 * tiles)] = linked[part][:, lanes]
                row = part * 2 * tiles + k * tiles + tile
                compressed_ref[pl.ds(row, 1)] = mine[part][:, lanes]


def run_finish(got):
    vmem = pl.BlockSpec(memory_space=pltpu.VMEM)
    return pl.pallas_call(
        finish_kernel,
        out_shape=(
            jax.ShapeDtypeStruct((2 * DATES * 12, 128), F32),
            jax.ShapeDtypeStruct((24, 128), F32),
        ),
        in_specs=[vmem],
        out_specs=(vmem, vmem),
        scratch_shapes=[pltpu.VMEM((512, 128), F32), pltpu.VMEM((ROWS, ROWS), BF16)],
        compiler_params=pltpu.CompilerParams(vmem_limit_bytes=20 * 1024 * 1024),
        name="finish",
    )(got)


def local(slc, owner_map):
    x = jnp.transpose(slc[:, 0], (1, 2, 0, 3))
    linked, compressed = run_finish(run_main(x, owner_map.reshape(1, BLOCKS)))
    return (
        linked.reshape(2, 1, DATES, 1, 2 * ROWS),
        compressed.reshape(2, 1, 1, 2 * ROWS),
    )


def solution(mesh):
    in_specs = (P(None, "stack", None, "pix", None), P())
    out_specs = (P(None, "stack", None, "pix", None), P(None, "stack", "pix", None))
    return jax.shard_map(local, mesh=mesh, in_specs=in_specs, out_specs=out_specs, check_vma=False)
```

```python
import math

import jax
import jax.numpy as jnp
from jax import lax
from jax.experimental import pallas as pl
from jax.experimental.pallas import tpu as pltpu
from jax.sharding import PartitionSpec as P

MESH = pl.DeviceIdType.MESH
F32, BF16, I32 = jnp.float32, jnp.bfloat16, jnp.int32
DATES, ITERS, SECT, ROWS, COLS, BLOCKS = 15, 8, 4, 768, 256, 128
STRIP = 6
UP = 5
TALL = 16
NY, NZ, NC = 4, 16, 2
GROUPS = NY * NC
FEAT = 32
XS = 24
NT_DIMS = (((1,), (1,)), ((), ()))


def place(y, z, c):
    return y * (NZ * NC) + z * NC + c


def iota(shape, dim):
    return lax.broadcasted_iota(I32, shape, dim)


def one_hot(mask):
    return jnp.where(mask, 1.0, 0.0).astype(BF16)


def unpack(src_ref, plain, k, rows):
    for t in range(DATES):
        for r in range(rows):
            pair = src_ref[t, r].astype(F32)
            row = (t * STRIP + r) * 2
            plain[k, 0, pl.ds(row, 2)] = pair[:, :128]
            plain[k, 1, pl.ds(row, 2)] = pair[:, 128:]


def spread(plain, k, r, row, x_ref, keep):
    for h in range(2):
        for comp in range(2):
            v = plain[k, h, pl.ds(r * 2 + comp, DATES, stride=STRIP * 2)]
            if keep is not None:
                v = jnp.where(keep, v, 0.0)
            x_ref[comp, h, pl.ds(row * XS, DATES)] = v
            x_ref[comp, h, pl.ds(row * XS + DATES, 8)] = v[:8]


def add(x, y):
    return tuple(p + q for p, q in zip(x, y))


def middle_sum(terms):
    total = terms(UP)
    for row in range(UP + 1, UP + STRIP):
        total = add(total, terms(row))
    return total


def window_sums(terms, middle):
    total = middle
    sums = [None] * STRIP
    sums[5] = total
    for row in range(4, -1, -1):
        total = add(total, terms(row))
        sums[row] = total
    tail = None
    for r in range(1, STRIP):
        term = terms(r + 10)
        tail = term if tail is None else add(tail, term)
        sums[r] = add(sums[r], tail)
    return sums


def split_store(ref, lead, row, h, value):
    high = value.astype(BF16)
    low = (value - high.astype(F32)).astype(BF16)
    ref[lead, pl.ds(row, 16), h * 128 : (h + 1) * 128] = high
    ref[lead, pl.ds(row, 16), 256 + h * 128 : 256 + (h + 1) * 128] = low


def products(x_ref, h, d):
    def power(row):
        re = x_ref[0, h, pl.ds(row * XS, 16)]
        im = x_ref[1, h, pl.ds(row * XS, 16)]
        return (re * re + im * im,)

    def product(row):
        are = x_ref[0, h, pl.ds(row * XS, 16)]
        aim = x_ref[1, h, pl.ds(row * XS, 16)]
        bre = x_ref[0, h, pl.ds(row * XS + d, 16)]
        bim = x_ref[1, h, pl.ds(row * XS + d, 16)]
        return (are * bre + aim * bim, aim * bre - are * bim)

    return product if d else power


def middles(x_ref, mid_ref):
    for d in range(8):
        for h in range(2):
            for part, value in enumerate(middle_sum(products(x_ref, h, d))):
                mid_ref[d, h, part] = value


def coherences(x_ref, mid_ref, sums_ref, band_ref, scale_ref, g_ref):
    for d in range(8):
        parts = 2 if d else 1
        for h in range(2):
            middle = tuple(mid_ref[d, h, part] for part in range(parts))
            for r, value in enumerate(window_sums(products(x_ref, h, d), middle)):
                for part in range(parts):
                    split_store(sums_ref, d, (r * parts + part) * 16, h, value[part])
        rows = STRIP * parts * 16
        summed = jnp.dot(sums_ref[d, :rows], band_ref[...], preferred_element_type=F32)
        if not d:
            scale = lax.rsqrt(summed + 1.0)
            for h in range(2):
                for r in range(STRIP):
                    v = scale[r * 16 : (r + 1) * 16, h * 128 : (h + 1) * 128]
                    scale_ref[h, pl.ds(r * XS, 16)] = v
                    scale_ref[h, pl.ds(r * XS + DATES, 8)] = v[:8]
            continue
        for h in range(2):
            for r in range(STRIP):
                both = scale_ref[h, pl.ds(r * XS, 16)] * scale_ref[h, pl.ds(r * XS + d, 16)]
                row = r * 32
                re = summed[row : row + 16, h * 128 : (h + 1) * 128] * both
                im = summed[row + 16 : row + 32, h * 128 : (h + 1) * 128] * both
                re, im = re.astype(BF16).astype(F32), im.astype(BF16).astype(F32)
                base = (d - 1) * 384 + r
                g_ref[h, pl.ds(base, 16, stride=8)] = re
                g_ref[h, pl.ds(base + 128, 16, stride=8)] = re + im
                g_ref[h, pl.ds(base + 256, 16, stride=8)] = im - re


def power_iterations(g_ref, plain, v_ref, c_ref):
    def at(a, b):
        d = (b - a) % DATES
        flip = d > 7
        if flip:
            a, d = b, DATES - d
        return (d - 1) * 384 + a * 8, flip

    def normalized(parts):
        energy = None
        for re, im in parts:
            term = re * re + im * im
            energy = term if energy is None else energy + term
        factor = lax.rsqrt(energy * (1.0 / DATES) + 0.25)
        return tuple((re * factor, im * factor) for re, im in parts)

    def half(h, _):
        first = []
        for a in range(DATES):
            re, im = jnp.ones((STRIP, 128), F32), jnp.zeros((STRIP, 128), F32)
            for b in range(DATES):
                if b != a:
                    base, flip = at(a, b)
                    gre = g_ref[h, pl.ds(base, STRIP)]
                    gim = g_ref[h, pl.ds(base + 128, STRIP)] - gre
                    re = re + gre
                    im = im - gim if flip else im + gim
            first.append((re, im))
        vec = normalized(first)

        def step(_, vec):
            both = [re + im for re, im in vec]
            out = []
            for a in range(DATES):
                one, two, three = None, None, None
                for b in range(DATES):
                    if b != a:
                        base, flip = at(a, b)
                        vre, vim = vec[b]
                        gre = g_ref[h, pl.ds(base, STRIP)]
                        plus = g_ref[h, pl.ds(base + 128, STRIP)]
                        minus = g_ref[h, pl.ds(base + 256, STRIP)]
                        p1 = gre * both[b]
                        one = p1 if one is None else one + p1
                        p2, p3 = (plus * vre, minus * vim) if flip else (minus * vre, plus * vim)
                        if two is None:
                            two, three = (-p2, -p3) if flip else (p2, p3)
                        elif flip:
                            two, three = two - p2, three - p3
                        else:
                            two, three = two + p2, three + p3
                out.append((vec[a][0] + (one - three), vec[a][1] + (one + two)))
            return normalized(out)

        vec = lax.fori_loop(0, ITERS - 1, step, vec)
        packed_re, packed_im = None, None
        for t in range(DATES):
            vre, vim = vec[t]
            sre = plain[0, h, pl.ds(t * STRIP * 2, STRIP, stride=2)]
            sim = plain[0, h, pl.ds(t * STRIP * 2 + 1, STRIP, stride=2)]
            re = vre * sre + vim * sim
            im = vre * sim - vim * sre
            packed_re = re if packed_re is None else packed_re + re
            packed_im = im if packed_im is None else packed_im + im
            v_ref[h, pl.ds(t * 8, STRIP)] = vre
            v_ref[h, pl.ds((16 + t) * 8, STRIP)] = vim
        norm = 1.0 / math.sqrt(DATES)
        c_ref[0, h] = packed_re * norm
        c_ref[1, h] = packed_im * norm
        return 0

    lax.fori_loop(0, 2, half, 0)


def main_kernel(
    x_hbm,
    map_hbm,
    out_ref,
    map_ref,
    x_ref,
    halo_ref,
    plain,
    x2_ref,
    mid_ref,
    sums_ref,
    band_ref,
    scale_ref,
    g_ref,
    v_ref,
    c_ref,
    pick_ref,
    rows_ref,
    rows2_ref,
    rows3_ref,
    send1,
    recv1,
    sendc,
    recvc,
    send2,
    recv2,
    sem_t,
    sem_x,
    sem_hs,
    sem_hr,
    sem_cs,
    sem_cr,
    sem_1s,
    sem_1r,
    sem_2s,
    sem_2r,
):
    section = lax.axis_index("stack")
    me = lax.axis_index("pix")
    y, rest = me // (NZ * NC), lax.rem(me, NZ * NC)
    z, c = rest // NC, lax.rem(rest, NC)
    g = y * NC + c

    sections = [lax.rem(section + o, SECT) for o in range(SECT)]
    group_of = [lax.rem(g + o, GROUPS) for o in range(GROUPS)]
    groups = [place(q // NC, z, lax.rem(q, NC)) for q in group_of]
    plane = [(s, o) for s in range(SECT) for o in range(GROUPS) if s or o]
    plane.sort(key=lambda so: -(min(so[0], 4 - so[0]) + min(so[1] // 2, 4 - so[1] // 2)))
    z_of = [lax.rem(z + o, NZ) for o in range(1, NZ)]
    depths = [place(y, q, c) for q in z_of]
    after, before = lax.rem(me + 1, BLOCKS), lax.rem(me + BLOCKS - 1, BLOCKS)
    other = lax.rem(me + BLOCKS + 2 * c - 1, BLOCKS)

    def device(s, o):
        return {"stack": sections[s], "pix": groups[o]}

    def at_x(o):
        return {"stack": lax.rem(section + o, SECT)}

    def at_y(o):
        return {"pix": place(lax.rem(y + o, NY), z, c)}

    def at_z(o):
        return {"pix": place(y, lax.rem(z + o, NZ), c)}

    at_core = {"pix": place(y, z, 1 - c)}
    nearest = [
        {"pix": other}, at_core, at_z(1), at_z(NZ - 1), at_y(1), at_y(NY - 1), at_x(1), at_x(SECT - 1)
    ]
    barrier = pltpu.get_barrier_semaphore()
    for peer in nearest:
        pl.semaphore_signal(barrier, inc=1, device_id=peer, device_id_type=MESH)

    def tell(sem, peers):
        for peer in peers:
            pl.semaphore_signal(sem, inc=1, device_id=peer, device_id_type=MESH)

    slots = pltpu.make_async_copy(map_hbm, map_ref, sem_x.at[0])
    slots.start()
    own = pltpu.make_async_copy(x_hbm, x_ref, sem_x.at[1])
    own.start()
    pl.semaphore_wait(barrier, len(nearest))

    sends = []

    def send(src, dst, ssem, rsem, device):
        copy = pltpu.make_async_remote_copy(
            src_ref=src, dst_ref=dst, send_sem=ssem, recv_sem=rsem,
            device_id=device, device_id_type=MESH,
        )
        copy.start()
        sends.append(copy)
        return copy

    halos = [
        send(x_hbm.at[:, 1:6], halo_ref.at[0], sem_hs.at[0], sem_hr.at[0], {"pix": after}),
        send(x_hbm.at[:, 0:5], halo_ref.at[1], sem_hs.at[1], sem_hr.at[1], {"pix": before}),
    ]

    tell(sem_t.at[0], [at_x(1)])
    tell(sem_t.at[1], [at_y(1)])
    tell(sem_t.at[2], [at_z(1), at_z(NZ - 1)])

    m = iota((128, 128), 0)
    slot = (m >> 5) * 32 + (m & 15) * 2 + ((m >> 4) & 1)
    slots.wait()
    owner = jnp.broadcast_to(map_ref[...], (128, 128))
    chosen = one_hot(slot == owner)
    column = iota((128, 256), 1)
    block = iota((128, 256), 0)
    for k in range(2):
        pick = jnp.dot(chosen, one_hot(column == 2 * block + k), preferred_element_type=F32)
        pick_ref[:, k * 256 : (k + 1) * 256] = pick.astype(BF16)
    band_ref[...] = one_hot(
        jnp.abs((iota((512, 256), 0) & 255) - iota((512, 256), 1)) <= 2
    )
    rows3_ref[...] = jnp.zeros((128, 512), F32)
    for h in range(2):
        for part in range(2):
            v_ref[h, pl.ds((part * 16 + DATES) * 8, 8)] = jnp.zeros((8, 128), F32)

    own.wait()
    unpack(x_ref, plain, 0, STRIP)
    for r in range(STRIP):
        spread(plain, 0, r, UP + r, x2_ref, None)
    middles(x2_ref, mid_ref)
    pl.semaphore_wait(sem_t.at[0], 1)
    pl.semaphore_wait(sem_t.at[1], 1)
    pl.semaphore_wait(sem_t.at[2], 2)
    tell(sem_t.at[3], [at_y(1), at_y(2), at_y(3)])
    tell(sem_t.at[4], [at_z(2), at_z(NZ - 2)])
    for copy in halos:
        copy.wait_recv()
    unpack(halo_ref.at[0], plain, 1, UP)
    unpack(halo_ref.at[1], plain, 2, UP)
    for r in range(UP):
        spread(plain, 1, r, r, x2_ref, me > 0)
        spread(plain, 2, r, UP + STRIP + r, x2_ref, me < BLOCKS - 1)
    coherences(x2_ref, mid_ref, sums_ref, band_ref, scale_ref, g_ref)
    pl.semaphore_wait(sem_t.at[3], 3)
    pl.semaphore_wait(sem_t.at[4], 2)
    tell(sem_t.at[5], [at_core])
    tell(sem_t.at[6], [at_z(4), at_z(NZ - 4)])
    power_iterations(g_ref, plain, v_ref, c_ref)
    pl.semaphore_wait(sem_t.at[5], 1)
    pl.semaphore_wait(sem_t.at[6], 2)

    for h in range(2):
        for comp in range(2):
            for k in range(2):
                at = pl.multiple_of(comp * 64 + k * 32 + section * 8, 8)
                lanes = slice(k * 256 + h * 128, k * 256 + (h + 1) * 128)
                rows3_ref[pl.ds(at, STRIP), lanes] = c_ref[comp, h]
    part = lax.dot_general(
        pick_ref[...], rows3_ref[...].astype(BF16), NT_DIMS, preferred_element_type=F32
    ).astype(BF16)
    for q in range(GROUPS):
        sendc[q] = part[q * 16 : (q + 1) * 16]
    first = [
        send(sendc.at[group_of[o]], recvc.at[section, g], sem_cs.at[s, o], sem_cr.at[s, o], device(s, o))
        for s, o in plane
    ]

    for h in range(2):
        lanes = slice(h * 128, (h + 1) * 128)
        for r in range(4):
            v = v_ref[h, pl.ds(r, FEAT, stride=8)].astype(BF16)
            rows_ref[r * FEAT : (r + 1) * FEAT, lanes] = v
        for r in range(2):
            v = v_ref[h, pl.ds(4 + r, FEAT, stride=8)].astype(BF16)
            for k in range(2):
                at = (k * 2 + r) * FEAT
                rows2_ref[at : at + FEAT, k * 256 + h * 128 : k * 256 + (h + 1) * 128] = v
                rows2_ref[at : at + FEAT, (1 - k) * 256 + h * 128 : (1 - k) * 256 + (h + 1) * 128] = (
                    jnp.zeros((FEAT, 128), BF16)
                )
    for k in range(2):
        part = lax.dot_general(
            pick_ref[:, k * 256 : (k + 1) * 256], rows_ref[...], NT_DIMS, preferred_element_type=F32
        ).astype(BF16)
        for q in range(GROUPS):
            send1[q, :, k * 128 : (k + 1) * 128] = part[q * 16 : (q + 1) * 16]
    part = lax.dot_general(
        pick_ref[...], rows2_ref[...], NT_DIMS, preferred_element_type=F32
    ).astype(BF16)
    for q in range(GROUPS):
        send1[q, :, 256:384] = part[q * 16 : (q + 1) * 16]
    second = [
        send(send1.at[group_of[o]], recv1.at[g], sem_1s.at[o], sem_1r.at[o], device(0, o))
        for s, o in plane
        if s == 0
    ]
    recvc[section, g] = sendc[g]
    recv1[g] = send1[g]
    i, j = iota((128, 128), 0), iota((128, 128), 1)
    turn = one_hot(j == (i & 7) * 16 + (i >> 3))
    for copy in first + second:
        copy.wait_recv()
    got = recv1[...].reshape(128, 384)
    moved = jnp.dot(turn, got, preferred_element_type=F32)
    for q in range(NZ):
        send2[q, :, :384] = moved[q * 8 : (q + 1) * 8].astype(BF16)
    packed = (recvc[0] + recvc[1] + recvc[2] + recvc[3]).reshape(128, 128)
    moved = jnp.dot(turn, packed, preferred_element_type=F32)
    for q in range(NZ):
        send2[q, :, 384:] = moved[q * 8 : (q + 1) * 8].astype(BF16)
    order = sorted(range(NZ - 1), key=lambda o: -min(o + 1, NZ - 1 - o))
    third = [
        send(send2.at[z_of[o]], recv2.at[z], sem_2s.at[o], sem_2r.at[o], {"pix": depths[o]})
        for o in order
    ]
    recv2[z] = send2[z]
    for copy in third:
        copy.wait_recv()
    out_ref[...] = recv2[...]
    for copy in sends:
        copy.wait_send()


def run_main(x, owner_map):
    vmem = pl.BlockSpec(memory_space=pltpu.VMEM)
    dma = pltpu.SemaphoreType.DMA
    return pl.pallas_call(
        main_kernel,
        out_shape=jax.ShapeDtypeStruct((NZ, GROUPS, 512), BF16),
        in_specs=[pl.BlockSpec(memory_space=pltpu.HBM)] * 2,
        out_specs=vmem,
        scratch_shapes=[
            pltpu.VMEM((1, BLOCKS), I32),
            pltpu.VMEM((DATES, STRIP, 2, COLS), BF16),
            pltpu.VMEM((2, DATES, UP, 2, COLS), BF16),
            pltpu.VMEM((3, 2, DATES * STRIP * 2, 128), F32),
            pltpu.VMEM((2, 2, TALL * XS, 128), F32),
            pltpu.VMEM((8, 2, 2, 16, 128), F32),
            pltpu.VMEM((8, STRIP * 32, 512), BF16),
            pltpu.VMEM((512, 256), BF16),
            pltpu.VMEM((2, STRIP * XS, 128), F32),
            pltpu.VMEM((2, 7 * 3 * 128, 128), F32),
            pltpu.VMEM((2, FEAT * 8, 128), F32),
            pltpu.VMEM((2, 2, STRIP, 128), F32),
            pltpu.VMEM((128, 512), BF16),
            pltpu.VMEM((128, 256), BF16),
            pltpu.VMEM((128, 512), BF16),
            pltpu.VMEM((128, 512), F32),
            pltpu.VMEM((GROUPS, NZ, 384), BF16),
            pltpu.VMEM((GROUPS, NZ, 384), BF16),
            pltpu.VMEM((GROUPS, NZ, 128), BF16),
            pltpu.VMEM((SECT, GROUPS, NZ, 128), BF16),
            pltpu.VMEM((NZ, GROUPS, 512), BF16),
            pltpu.VMEM((NZ, GROUPS, 512), BF16),
            pltpu.SemaphoreType.REGULAR((7,)),
            dma((2,)),
            dma((2,)),
            dma((2,)),
            dma((SECT, GROUPS)),
            dma((SECT, GROUPS)),
            dma((GROUPS,)),
            dma((GROUPS,)),
            dma((NZ - 1,)),
            dma((NZ - 1,)),
        ],
        compiler_params=pltpu.CompilerParams(
            collective_id=0, has_side_effects=True, vmem_limit_bytes=20 * 1024 * 1024
        ),
        name="link",
    )(x, owner_map)


def finish_kernel(got_ref, linked_ref, compressed_ref, turned_ref, spread_ref):
    section = lax.axis_index("stack")
    n, lane = iota((128, ROWS), 0), iota((128, ROWS), 1)
    strip = ((n >> 1) & 3) * 32 + (n >> 3) * 2 + (n & 1)
    for r in range(STRIP):
        spread_ref[r * 128 : (r + 1) * 128] = one_hot(lane == strip * STRIP + r)
    got = jnp.concatenate([got_ref[q].astype(F32) for q in range(NZ)], axis=0)
    for tile in range(4):
        turned_ref[tile * 128 : (tile + 1) * 128] = got[:, tile * 128 : (tile + 1) * 128].T
    blocks = []
    for k in range(2):
        pieces = []
        for r in range(STRIP):
            at = k * 128 + r * FEAT if r < 4 else 256 + (k * 2 + r - 4) * FEAT
            pieces.append(turned_ref[pl.ds(at, FEAT)].astype(BF16))
        blocks.append(jnp.concatenate(pieces, axis=1))
    pieces = []
    for r in range(STRIP):
        pair = [turned_ref[pl.ds(384 + comp * 64 + r, 8, stride=8)] for comp in range(2)]
        pieces.append(jnp.concatenate(pair, axis=0).astype(BF16))
    blocks.append(jnp.concatenate(pieces, axis=1))
    out = jnp.dot(jnp.concatenate(blocks, axis=0), spread_ref[...], preferred_element_type=F32)
    re, im = out[64:72], out[72:80]
    link_re = re[1:] * re[:-1] + im[1:] * im[:-1]
    link_im = im[1:] * re[:-1] - re[1:] * im[:-1]
    factor = lax.rsqrt(link_re * link_re + link_im * link_im + 1.0)
    unit_re, unit_im = link_re * factor, link_im * factor
    tiles = ROWS // 128
    for k in range(2):
        datum_re, datum_im = jnp.ones((1, ROWS), F32), jnp.zeros((1, ROWS), F32)
        mine_re, mine_im = re[k * 4 : k * 4 + 1], im[k * 4 : k * 4 + 1]
        for j in range(SECT - 1):
            at = k * 4 + j
            ure, uim = unit_re[at : at + 1], unit_im[at : at + 1]
            new_re = datum_re * ure - datum_im * uim
            new_im = datum_re * uim + datum_im * ure
            reached = j < section
            datum_re = jnp.where(reached, new_re, datum_re)
            datum_im = jnp.where(reached, new_im, datum_im)
            mine_re = jnp.where(reached, re[at + 1 : at + 2], mine_re)
            mine_im = jnp.where(reached, im[at + 1 : at + 2], mine_im)
        at = k * FEAT
        vre, vim = out[at : at + DATES], out[at + 16 : at + 16 + DATES]
        linked = (vre * datum_re - vim * datum_im, vre * datum_im + vim * datum_re)
        mine = (mine_re, mine_im)
        for part in range(2):
            for tile in range(tiles):
                row = part * DATES * 2 * tiles + k * tiles + tile
                lanes = slice(tile * 128, (tile + 1) * 128)
                linked_ref[pl.ds(row, DATES, stride=2 * tiles)] = linked[part][:, lanes]
                row = part * 2 * tiles + k * tiles + tile
                compressed_ref[pl.ds(row, 1)] = mine[part][:, lanes]


def run_finish(got):
    vmem = pl.BlockSpec(memory_space=pltpu.VMEM)
    return pl.pallas_call(
        finish_kernel,
        out_shape=(
            jax.ShapeDtypeStruct((2 * DATES * 12, 128), F32),
            jax.ShapeDtypeStruct((24, 128), F32),
        ),
        in_specs=[vmem],
        out_specs=(vmem, vmem),
        scratch_shapes=[pltpu.VMEM((512, 128), F32), pltpu.VMEM((ROWS, ROWS), BF16)],
        compiler_params=pltpu.CompilerParams(vmem_limit_bytes=20 * 1024 * 1024),
        name="finish",
    )(got)


def local(slc, owner_map):
    x = jnp.transpose(slc[:, 0], (1, 2, 0, 3))
    linked, compressed = run_finish(run_main(pltpu.with_memory_space_constraint(x, pltpu.HBM), pltpu.with_memory_space_constraint(owner_map.reshape(1, BLOCKS), pltpu.HBM)))
    return (
        linked.reshape(2, 1, DATES, 1, 2 * ROWS),
        compressed.reshape(2, 1, 1, 2 * ROWS),
    )


def solution(mesh):
    in_specs = (P(None, "stack", None, "pix", None), P())
    out_specs = (P(None, "stack", None, "pix", None), P(None, "stack", "pix", None))
    return jax.shard_map(local, mesh=mesh, in_specs=in_specs, out_specs=out_specs, check_vma=False)
```

```python
import math

import jax
import jax.numpy as jnp
from jax import lax
from jax.experimental import pallas as pl
from jax.experimental.pallas import tpu as pltpu
from jax.sharding import PartitionSpec as P

MESH = pl.DeviceIdType.MESH
F32, BF16, I32 = jnp.float32, jnp.bfloat16, jnp.int32
DATES, ITERS, SECT, ROWS, COLS, BLOCKS = 15, 8, 4, 768, 256, 128
STRIP = 6
UP = 5
TALL = 16
NY, NZ, NC = 4, 16, 2
GROUPS = NY * NC
FEAT = 32
XS = 24
NT_DIMS = (((1,), (1,)), ((), ()))


def place(y, z, c):
    return y * (NZ * NC) + z * NC + c


def iota(shape, dim):
    return lax.broadcasted_iota(I32, shape, dim)


def one_hot(mask):
    return jnp.where(mask, 1.0, 0.0).astype(BF16)


def unpack(src_ref, plain, k, rows):
    for t in range(DATES):
        for r in range(rows):
            pair = src_ref[t, r].astype(F32)
            row = (t * STRIP + r) * 2
            plain[k, 0, pl.ds(row, 2)] = pair[:, :128]
            plain[k, 1, pl.ds(row, 2)] = pair[:, 128:]


def spread(plain, k, r, row, x_ref, keep):
    for h in range(2):
        for comp in range(2):
            v = plain[k, h, pl.ds(r * 2 + comp, DATES, stride=STRIP * 2)]
            if keep is not None:
                v = jnp.where(keep, v, 0.0)
            x_ref[comp, h, pl.ds(row * XS, DATES)] = v
            x_ref[comp, h, pl.ds(row * XS + DATES, 8)] = v[:8]


def add(x, y):
    return tuple(p + q for p, q in zip(x, y))


def middle_sum(terms):
    total = terms(UP)
    for row in range(UP + 1, UP + STRIP):
        total = add(total, terms(row))
    return total


def window_sums(terms, middle):
    total = middle
    sums = [None] * STRIP
    sums[5] = total
    for row in range(4, -1, -1):
        total = add(total, terms(row))
        sums[row] = total
    tail = None
    for r in range(1, STRIP):
        term = terms(r + 10)
        tail = term if tail is None else add(tail, term)
        sums[r] = add(sums[r], tail)
    return sums


def split_store(ref, lead, row, h, value):
    high = value.astype(BF16)
    low = (value - high.astype(F32)).astype(BF16)
    ref[lead, pl.ds(row, 16), h * 128 : (h + 1) * 128] = high
    ref[lead, pl.ds(row, 16), 256 + h * 128 : 256 + (h + 1) * 128] = low


def products(x_ref, h, d):
    def power(row):
        re = x_ref[0, h, pl.ds(row * XS, 16)]
        im = x_ref[1, h, pl.ds(row * XS, 16)]
        return (re * re + im * im,)

    def product(row):
        are = x_ref[0, h, pl.ds(row * XS, 16)]
        aim = x_ref[1, h, pl.ds(row * XS, 16)]
        bre = x_ref[0, h, pl.ds(row * XS + d, 16)]
        bim = x_ref[1, h, pl.ds(row * XS + d, 16)]
        return (are * bre + aim * bim, aim * bre - are * bim)

    return product if d else power


def middles(x_ref, mid_ref):
    for d in range(8):
        for h in range(2):
            for part, value in enumerate(middle_sum(products(x_ref, h, d))):
                mid_ref[d, h, part] = value


def coherences(x_ref, mid_ref, sums_ref, band_ref, scale_ref, g_ref):
    for d in range(8):
        parts = 2 if d else 1
        for h in range(2):
            middle = tuple(mid_ref[d, h, part] for part in range(parts))
            for r, value in enumerate(window_sums(products(x_ref, h, d), middle)):
                for part in range(parts):
                    split_store(sums_ref, d, (r * parts + part) * 16, h, value[part])
        rows = STRIP * parts * 16
        summed = jnp.dot(sums_ref[d, :rows], band_ref[...], preferred_element_type=F32)
        if not d:
            scale = lax.rsqrt(summed + 1.0)
            for h in range(2):
                for r in range(STRIP):
                    v = scale[r * 16 : (r + 1) * 16, h * 128 : (h + 1) * 128]
                    scale_ref[h, pl.ds(r * XS, 16)] = v
                    scale_ref[h, pl.ds(r * XS + DATES, 8)] = v[:8]
            continue
        for h in range(2):
            for r in range(STRIP):
                both = scale_ref[h, pl.ds(r * XS, 16)] * scale_ref[h, pl.ds(r * XS + d, 16)]
                row = r * 32
                re = summed[row : row + 16, h * 128 : (h + 1) * 128] * both
                im = summed[row + 16 : row + 32, h * 128 : (h + 1) * 128] * both
                re, im = re.astype(BF16).astype(F32), im.astype(BF16).astype(F32)
                base = (d - 1) * 384 + r
                g_ref[h, pl.ds(base, 16, stride=8)] = re
                g_ref[h, pl.ds(base + 128, 16, stride=8)] = re + im
                g_ref[h, pl.ds(base + 256, 16, stride=8)] = im - re


def power_iterations(g_ref, plain, v_ref, c_ref):
    def at(a, b):
        d = (b - a) % DATES
        flip = d > 7
        if flip:
            a, d = b, DATES - d
        return (d - 1) * 384 + a * 8, flip

    def energy(parts):
        total = None
        for re, im in parts:
            term = re * re + im * im
            total = term if total is None else total + term
        return total

    def rescaled(scale, parts):
        return scale * lax.rsqrt(scale * scale * energy(parts) * (1.0 / DATES) + 0.25)

    def half(h, _):
        first = []
        for a in range(DATES):
            re, im = jnp.ones((STRIP, 128), F32), jnp.zeros((STRIP, 128), F32)
            for b in range(DATES):
                if b != a:
                    base, flip = at(a, b)
                    gre = g_ref[h, pl.ds(base, STRIP)]
                    gim = g_ref[h, pl.ds(base + 128, STRIP)] - gre
                    re = re + gre
                    im = im - gim if flip else im + gim
            first.append((re, im))

        def step(_, carry):
            vec, scale = carry
            scale = rescaled(scale, vec)
            both = [re + im for re, im in vec]
            def matvec(a, first, second, ops):
                total = None
                for step in range(1, DATES):
                    b = (a + step) % DATES
                    base, flip = at(a, b)
                    term = g_ref[h, pl.ds(base + (second if flip else first), STRIP)] * ops[b]
                    if total is None:
                        total = term
                    else:
                        total = total - term if flip and first else total + term
                return total

            ones = [matvec(a, 0, 0, both) for a in range(DATES)]
            twos = [ones[a] + matvec(a, 256, 128, [v[0] for v in vec]) for a in range(DATES)]
            out = []
            for a in range(DATES):
                three = matvec(a, 128, 256, [v[1] for v in vec])
                out.append((vec[a][0] + (ones[a] - three), vec[a][1] + twos[a]))
            return tuple(out), scale

        carry = (tuple(first), jnp.ones((STRIP, 128), F32))
        vec, scale = lax.fori_loop(0, ITERS - 1, step, carry, unroll=True)
        scale = rescaled(scale, vec)
        vec = [(re * scale, im * scale) for re, im in vec]
        packed_re, packed_im = None, None
        for t in range(DATES):
            vre, vim = vec[t]
            sre = plain[0, h, pl.ds(t * STRIP * 2, STRIP, stride=2)]
            sim = plain[0, h, pl.ds(t * STRIP * 2 + 1, STRIP, stride=2)]
            re = vre * sre + vim * sim
            im = vre * sim - vim * sre
            packed_re = re if packed_re is None else packed_re + re
            packed_im = im if packed_im is None else packed_im + im
            v_ref[h, pl.ds(t * 8, STRIP)] = vre
            v_ref[h, pl.ds((16 + t) * 8, STRIP)] = vim
        norm = 1.0 / math.sqrt(DATES)
        c_ref[0, h] = packed_re * norm
        c_ref[1, h] = packed_im * norm
        return 0

    lax.fori_loop(0, 2, half, 0)


def main_kernel(
    x_hbm,
    map_hbm,
    out_ref,
    spread_ref,
    map_ref,
    x_ref,
    halo_ref,
    plain,
    x2_ref,
    mid_ref,
    sums_ref,
    band_ref,
    scale_ref,
    g_ref,
    v_ref,
    c_ref,
    pick_ref,
    rows_ref,
    rows2_ref,
    rows3_ref,
    send1,
    recv1,
    sendc,
    recvc,
    send2,
    recv2,
    sem_t,
    sem_x,
    sem_hs,
    sem_hr,
    sem_cs,
    sem_cr,
    sem_1s,
    sem_1r,
    sem_2s,
    sem_2r,
):
    section = lax.axis_index("stack")
    me = lax.axis_index("pix")
    y, rest = lax.div(me, NZ * NC), lax.rem(me, NZ * NC)
    z, c = lax.div(rest, NC), lax.rem(rest, NC)
    other = lax.rem(me + BLOCKS + 2 * c - 1, BLOCKS)

    def at_x(o):
        return {"stack": lax.rem(section + o, SECT)}

    def at_y(o):
        return {"pix": place(lax.rem(y + o, NY), z, c)}

    def at_z(o):
        return {"pix": place(y, lax.rem(z + o, NZ), c)}

    at_core = {"pix": place(y, z, 1 - c)}
    nearest = [
        {"pix": other}, at_core, at_z(1), at_z(NZ - 1), at_y(1), at_y(NY - 1), at_x(1), at_x(SECT - 1)
    ]
    barrier = pltpu.get_barrier_semaphore()
    for peer in nearest:
        pl.semaphore_signal(barrier, inc=1, device_id=peer, device_id_type=MESH)

    def tell(sem, peers):
        for peer in peers:
            pl.semaphore_signal(sem, inc=1, device_id=peer, device_id_type=MESH)

    slots = pltpu.make_async_copy(map_hbm, map_ref, sem_x.at[0])
    slots.start()
    own = pltpu.make_async_copy(x_hbm, x_ref, sem_x.at[1])
    own.start()
    pl.semaphore_wait(barrier, len(nearest))

    sends = []

    def send(src, dst, ssem, rsem, device):
        copy = pltpu.make_async_remote_copy(
            src_ref=src, dst_ref=dst, send_sem=ssem, recv_sem=rsem,
            device_id=device, device_id_type=MESH,
        )
        copy.start()
        sends.append(copy)
        return copy

    after, before = lax.rem(me + 1, BLOCKS), lax.rem(me + BLOCKS - 1, BLOCKS)
    halos = [
        send(x_hbm.at[:, 1:6], halo_ref.at[0], sem_hs.at[0], sem_hr.at[0], {"pix": after}),
        send(x_hbm.at[:, 0:5], halo_ref.at[1], sem_hs.at[1], sem_hr.at[1], {"pix": before}),
    ]

    tell(sem_t.at[0], [at_x(1)])
    tell(sem_t.at[1], [at_y(1)])
    tell(sem_t.at[2], [at_z(1), at_z(NZ - 1)])

    g = y * NC + c
    group_of = [lax.rem(g + o, GROUPS) for o in range(GROUPS)]
    groups = [place(lax.div(q, NC), z, lax.rem(q, NC)) for q in group_of]
    far = sorted(range(GROUPS), key=lambda o: -min(o // 2, 4 - o // 2))
    z_of = [lax.rem(z + o, NZ) for o in range(1, NZ)]
    depths = [place(y, q, c) for q in z_of]

    m = iota((128, 128), 0)
    slot = (m >> 5) * 32 + (m & 15) * 2 + ((m >> 4) & 1)
    slots.wait()
    owner = jnp.broadcast_to(map_ref[...], (128, 128))
    chosen = one_hot(slot == owner)
    column = iota((128, 256), 1)
    block = iota((128, 256), 0)
    for k in range(2):
        pick = jnp.dot(chosen, one_hot(column == 2 * block + k), preferred_element_type=F32)
        pick_ref[:, k * 256 : (k + 1) * 256] = pick.astype(BF16)
    band_ref[...] = one_hot(
        jnp.abs((iota((512, 256), 0) & 255) - iota((512, 256), 1)) <= 2
    )
    rows3_ref[...] = jnp.zeros((128, 512), F32)
    for h in range(2):
        for part in range(2):
            v_ref[h, pl.ds((part * 16 + DATES) * 8, 8)] = jnp.zeros((8, 128), F32)

    own.wait()
    unpack(x_ref, plain, 0, STRIP)
    for r in range(STRIP):
        spread(plain, 0, r, UP + r, x2_ref, None)
    middles(x2_ref, mid_ref)
    pl.semaphore_wait(sem_t.at[0], 1)
    pl.semaphore_wait(sem_t.at[1], 1)
    pl.semaphore_wait(sem_t.at[2], 2)
    tell(sem_t.at[3], [at_y(1), at_y(2), at_y(3)])
    tell(sem_t.at[4], [at_z(2), at_z(NZ - 2)])
    for copy in halos:
        copy.wait_recv()
    unpack(halo_ref.at[0], plain, 1, UP)
    unpack(halo_ref.at[1], plain, 2, UP)
    for r in range(UP):
        spread(plain, 1, r, r, x2_ref, me > 0)
        spread(plain, 2, r, UP + STRIP + r, x2_ref, me < BLOCKS - 1)
    coherences(x2_ref, mid_ref, sums_ref, band_ref, scale_ref, g_ref)
    pl.semaphore_wait(sem_t.at[3], 3)
    pl.semaphore_wait(sem_t.at[4], 2)
    tell(sem_t.at[5], [at_core])
    tell(sem_t.at[6], [at_z(4), at_z(NZ - 4)])
    power_iterations(g_ref, plain, v_ref, c_ref)
    pl.semaphore_wait(sem_t.at[5], 1)
    pl.semaphore_wait(sem_t.at[6], 2)

    for h in range(2):
        for comp in range(2):
            for k in range(2):
                at = pl.multiple_of(comp * 64 + k * 32 + section * 8, 8)
                lanes = slice(k * 256 + h * 128, k * 256 + (h + 1) * 128)
                rows3_ref[pl.ds(at, STRIP), lanes] = c_ref[comp, h]
    part = lax.dot_general(
        pick_ref[...], rows3_ref[...].astype(BF16), NT_DIMS, preferred_element_type=F32
    ).astype(BF16)
    for q in range(GROUPS):
        sendc[q] = part[q * 16 : (q + 1) * 16]
    def later(s, o):
        return pltpu.make_async_remote_copy(
            src_ref=sendc.at[group_of[o]], dst_ref=recvc.at[section, g],
            send_sem=sem_cs.at[s, o], recv_sem=sem_cr.at[s, o],
            device_id={"stack": section + s, "pix": groups[o]}, device_id_type=MESH,
        )

    for s in (2, 3, 1):

        @pl.when(section + s < SECT)
        def _():
            for o in far:
                later(s, o).start()

    here = [
        send(sendc.at[group_of[o]], recvc.at[section, g], sem_cs.at[0, o], sem_cr.at[0, o], {"pix": groups[o]})
        for o in far
        if o
    ]

    for h in range(2):
        lanes = slice(h * 128, (h + 1) * 128)
        for r in range(4):
            v = v_ref[h, pl.ds(r, FEAT, stride=8)].astype(BF16)
            rows_ref[r * FEAT : (r + 1) * FEAT, lanes] = v
        for r in range(2):
            v = v_ref[h, pl.ds(4 + r, FEAT, stride=8)].astype(BF16)
            for k in range(2):
                at = (k * 2 + r) * FEAT
                rows2_ref[at : at + FEAT, k * 256 + h * 128 : k * 256 + (h + 1) * 128] = v
                rows2_ref[at : at + FEAT, (1 - k) * 256 + h * 128 : (1 - k) * 256 + (h + 1) * 128] = (
                    jnp.zeros((FEAT, 128), BF16)
                )
    for k in range(2):
        part = lax.dot_general(
            pick_ref[:, k * 256 : (k + 1) * 256], rows_ref[...], NT_DIMS, preferred_element_type=F32
        ).astype(BF16)
        for q in range(GROUPS):
            send1[q, :, k * 128 : (k + 1) * 128] = part[q * 16 : (q + 1) * 16]
    part = lax.dot_general(
        pick_ref[...], rows2_ref[...], NT_DIMS, preferred_element_type=F32
    ).astype(BF16)
    for q in range(GROUPS):
        send1[q, :, 256:384] = part[q * 16 : (q + 1) * 16]
    here += [
        send(send1.at[group_of[o]], recv1.at[g], sem_1s.at[o], sem_1r.at[o], {"pix": groups[o]})
        for o in far
        if o
    ]
    recvc[section, g] = sendc[g]
    recv1[g] = send1[g]
    i, j = iota((128, 128), 0), iota((128, 128), 1)
    turn = one_hot(j == (i & 7) * 16 + (i >> 3))
    for copy in here:
        copy.wait_recv()
    for s in range(1, SECT):

        @pl.when(section >= s)
        def _():
            for o in range(GROUPS):
                later(s, o).wait_recv()

    got = recv1[...].reshape(128, 384)
    moved = jnp.dot(turn, got, preferred_element_type=F32)
    for q in range(NZ):
        send2[q, :, :384] = moved[q * 8 : (q + 1) * 8].astype(BF16)
    packed = recvc[0]
    for s in range(1, SECT):
        packed = jnp.where(section >= s, packed + recvc[s], packed)
    packed = packed.reshape(128, 128)
    moved = jnp.dot(turn, packed, preferred_element_type=F32)
    for q in range(NZ):
        send2[q, :, 384:] = moved[q * 8 : (q + 1) * 8].astype(BF16)
    order = sorted(range(NZ - 1), key=lambda o: -min(o + 1, NZ - 1 - o))
    third = [
        send(send2.at[z_of[o]], recv2.at[z], sem_2s.at[o], sem_2r.at[o], {"pix": depths[o]})
        for o in order
    ]
    recv2[z] = send2[z]
    n, lane = iota((128, ROWS), 0), iota((128, ROWS), 1)
    strip = ((n >> 1) & 3) * 32 + (n >> 3) * 2 + (n & 1)
    for r in range(STRIP):
        spread_ref[r * 128 : (r + 1) * 128] = one_hot(lane == strip * STRIP + r)
    for copy in third:
        copy.wait_recv()
    out_ref[...] = recv2[...]
    for copy in sends:
        copy.wait_send()
    for s in range(1, SECT):

        @pl.when(section + s < SECT)
        def _():
            for o in range(GROUPS):
                later(s, o).wait_send()


def run_main(x, owner_map):
    vmem = pl.BlockSpec(memory_space=pltpu.VMEM)
    dma = pltpu.SemaphoreType.DMA
    return pl.pallas_call(
        main_kernel,
        out_shape=(
            jax.ShapeDtypeStruct((NZ, GROUPS, 512), BF16),
            jax.ShapeDtypeStruct((ROWS, ROWS), BF16),
        ),
        in_specs=[pl.BlockSpec(memory_space=pltpu.HBM)] * 2,
        out_specs=(vmem, vmem),
        scratch_shapes=[
            pltpu.VMEM((1, BLOCKS), I32),
            pltpu.VMEM((DATES, STRIP, 2, COLS), BF16),
            pltpu.VMEM((2, DATES, UP, 2, COLS), BF16),
            pltpu.VMEM((3, 2, DATES * STRIP * 2, 128), F32),
            pltpu.VMEM((2, 2, TALL * XS, 128), F32),
            pltpu.VMEM((8, 2, 2, 16, 128), F32),
            pltpu.VMEM((8, STRIP * 32, 512), BF16),
            pltpu.VMEM((512, 256), BF16),
            pltpu.VMEM((2, STRIP * XS, 128), F32),
            pltpu.VMEM((2, 7 * 3 * 128, 128), F32),
            pltpu.VMEM((2, FEAT * 8, 128), F32),
            pltpu.VMEM((2, 2, STRIP, 128), F32),
            pltpu.VMEM((128, 512), BF16),
            pltpu.VMEM((128, 256), BF16),
            pltpu.VMEM((128, 512), BF16),
            pltpu.VMEM((128, 512), F32),
            pltpu.VMEM((GROUPS, NZ, 384), BF16),
            pltpu.VMEM((GROUPS, NZ, 384), BF16),
            pltpu.VMEM((GROUPS, NZ, 128), BF16),
            pltpu.VMEM((SECT, GROUPS, NZ, 128), BF16),
            pltpu.VMEM((NZ, GROUPS, 512), BF16),
            pltpu.VMEM((NZ, GROUPS, 512), BF16),
            pltpu.SemaphoreType.REGULAR((7,)),
            dma((2,)),
            dma((2,)),
            dma((2,)),
            dma((SECT, GROUPS)),
            dma((SECT, GROUPS)),
            dma((GROUPS,)),
            dma((GROUPS,)),
            dma((NZ - 1,)),
            dma((NZ - 1,)),
        ],
        compiler_params=pltpu.CompilerParams(
            collective_id=0, has_side_effects=True, vmem_limit_bytes=20 * 1024 * 1024
        ),
        name="link",
    )(x, owner_map)


def finish_kernel(got_ref, spread_ref, linked_ref, compressed_ref, turned_ref):
    section = lax.axis_index("stack")
    got = jnp.concatenate([got_ref[q].astype(F32) for q in range(NZ)], axis=0)
    for tile in range(4):
        turned_ref[tile * 128 : (tile + 1) * 128] = got[:, tile * 128 : (tile + 1) * 128].T
    blocks = []
    for k in range(2):
        pieces = []
        for r in range(STRIP):
            at = k * 128 + r * FEAT if r < 4 else 256 + (k * 2 + r - 4) * FEAT
            pieces.append(turned_ref[pl.ds(at, FEAT)].astype(BF16))
        blocks.append(jnp.concatenate(pieces, axis=1))
    pieces = []
    for r in range(STRIP):
        pair = [turned_ref[pl.ds(384 + comp * 64 + r, 8, stride=8)] for comp in range(2)]
        pieces.append(jnp.concatenate(pair, axis=0).astype(BF16))
    blocks.append(jnp.concatenate(pieces, axis=1))
    out = jnp.dot(jnp.concatenate(blocks, axis=0), spread_ref[...], preferred_element_type=F32)
    re, im = out[64:72], out[72:80]
    link_re = re[1:] * re[:-1] + im[1:] * im[:-1]
    link_im = im[1:] * re[:-1] - re[1:] * im[:-1]
    factor = lax.rsqrt(link_re * link_re + link_im * link_im + 1.0)
    unit_re, unit_im = link_re * factor, link_im * factor
    tiles = ROWS // 128
    for k in range(2):
        datum_re, datum_im = jnp.ones((1, ROWS), F32), jnp.zeros((1, ROWS), F32)
        mine_re, mine_im = re[k * 4 : k * 4 + 1], im[k * 4 : k * 4 + 1]
        for j in range(SECT - 1):
            at = k * 4 + j
            ure, uim = unit_re[at : at + 1], unit_im[at : at + 1]
            new_re = datum_re * ure - datum_im * uim
            new_im = datum_re * uim + datum_im * ure
            reached = j < section
            datum_re = jnp.where(reached, new_re, datum_re)
            datum_im = jnp.where(reached, new_im, datum_im)
            mine_re = jnp.where(reached, re[at + 1 : at + 2], mine_re)
            mine_im = jnp.where(reached, im[at + 1 : at + 2], mine_im)
        at = k * FEAT
        vre, vim = out[at : at + DATES], out[at + 16 : at + 16 + DATES]
        linked = (vre * datum_re - vim * datum_im, vre * datum_im + vim * datum_re)
        mine = (mine_re, mine_im)
        for part in range(2):
            for tile in range(tiles):
                row = part * DATES * 2 * tiles + k * tiles + tile
                lanes = slice(tile * 128, (tile + 1) * 128)
                linked_ref[pl.ds(row, DATES, stride=2 * tiles)] = linked[part][:, lanes]
                row = part * 2 * tiles + k * tiles + tile
                compressed_ref[pl.ds(row, 1)] = mine[part][:, lanes]


def run_finish(got, spread):
    vmem = pl.BlockSpec(memory_space=pltpu.VMEM)
    return pl.pallas_call(
        finish_kernel,
        out_shape=(
            jax.ShapeDtypeStruct((2 * DATES * 12, 128), F32),
            jax.ShapeDtypeStruct((24, 128), F32),
        ),
        in_specs=[vmem, vmem],
        out_specs=(vmem, vmem),
        scratch_shapes=[pltpu.VMEM((512, 128), F32)],
        compiler_params=pltpu.CompilerParams(vmem_limit_bytes=20 * 1024 * 1024),
        name="finish",
    )(got, spread)


def local(slc, owner_map):
    x = jnp.transpose(slc[:, 0], (1, 2, 0, 3))
    linked, compressed = run_finish(*run_main(pltpu.with_memory_space_constraint(x, pltpu.HBM), pltpu.with_memory_space_constraint(owner_map.reshape(1, BLOCKS), pltpu.HBM)))
    return (
        linked.reshape(2, 1, DATES, 1, 2 * ROWS),
        compressed.reshape(2, 1, 1, 2 * ROWS),
    )


def solution(mesh):
    in_specs = (P(None, "stack", None, "pix", None), P())
    out_specs = (P(None, "stack", None, "pix", None), P(None, "stack", "pix", None))
    return jax.shard_map(local, mesh=mesh, in_specs=in_specs, out_specs=out_specs, check_vma=False)
```

```python
import math

import jax
import jax.numpy as jnp
from jax import lax
from jax.experimental import pallas as pl
from jax.experimental.pallas import tpu as pltpu
from jax.sharding import PartitionSpec as P

MESH = pl.DeviceIdType.MESH
F32, BF16, I32 = jnp.float32, jnp.bfloat16, jnp.int32
DATES, ITERS, SECT, ROWS, COLS, BLOCKS = 15, 8, 4, 768, 256, 128
STRIP = 6
UP = 5
TALL = 16
NY, NZ, NC = 4, 16, 2
GROUPS = NY * NC
FEAT = 32
XS = 24
NT_DIMS = (((1,), (1,)), ((), ()))


def place(y, z, c):
    return y * (NZ * NC) + z * NC + c


def iota(shape, dim):
    return lax.broadcasted_iota(I32, shape, dim)


def one_hot(mask):
    return jnp.where(mask, 1.0, 0.0).astype(BF16)


def unpack(src_ref, plain, k, rows):
    for t in range(DATES):
        for r in range(rows):
            pair = src_ref[t, r].astype(F32)
            row = (t * STRIP + r) * 2
            plain[k, 0, pl.ds(row, 2)] = pair[:, :128]
            plain[k, 1, pl.ds(row, 2)] = pair[:, 128:]


def spread(plain, k, r, row, x_ref, keep):
    for h in range(2):
        for comp in range(2):
            v = plain[k, h, pl.ds(r * 2 + comp, DATES, stride=STRIP * 2)]
            if keep is not None:
                v = jnp.where(keep, v, 0.0)
            x_ref[comp, h, pl.ds(row * XS, DATES)] = v
            x_ref[comp, h, pl.ds(row * XS + DATES, 8)] = v[:8]


def add(x, y):
    return tuple(p + q for p, q in zip(x, y))


def middle_sum(terms):
    total = terms(UP)
    for row in range(UP + 1, UP + STRIP):
        total = add(total, terms(row))
    return total


def window_sums(terms, middle):
    total = middle
    sums = [None] * STRIP
    sums[5] = total
    for row in range(4, -1, -1):
        total = add(total, terms(row))
        sums[row] = total
    tail = None
    for r in range(1, STRIP):
        term = terms(r + 10)
        tail = term if tail is None else add(tail, term)
        sums[r] = add(sums[r], tail)
    return sums


def split_store(ref, lead, row, h, value):
    high = value.astype(BF16)
    low = (value - high.astype(F32)).astype(BF16)
    ref[lead, pl.ds(row, 16), h * 128 : (h + 1) * 128] = high
    ref[lead, pl.ds(row, 16), 256 + h * 128 : 256 + (h + 1) * 128] = low


def products(x_ref, h, d):
    def power(row):
        re = x_ref[0, h, pl.ds(row * XS, 16)]
        im = x_ref[1, h, pl.ds(row * XS, 16)]
        return (re * re + im * im,)

    def product(row):
        are = x_ref[0, h, pl.ds(row * XS, 16)]
        aim = x_ref[1, h, pl.ds(row * XS, 16)]
        bre = x_ref[0, h, pl.ds(row * XS + d, 16)]
        bim = x_ref[1, h, pl.ds(row * XS + d, 16)]
        return (are * bre + aim * bim, aim * bre - are * bim)

    return product if d else power


def middles(x_ref, mid_ref):
    for d in range(8):
        for h in range(2):
            for part, value in enumerate(middle_sum(products(x_ref, h, d))):
                mid_ref[d, h, part] = value


def coherences(x_ref, mid_ref, sums_ref, band_ref, scale_ref, g_ref):
    for d in range(8):
        parts = 2 if d else 1
        for h in range(2):
            middle = tuple(mid_ref[d, h, part] for part in range(parts))
            for r, value in enumerate(window_sums(products(x_ref, h, d), middle)):
                for part in range(parts):
                    split_store(sums_ref, d, (r * parts + part) * 16, h, value[part])
        rows = STRIP * parts * 16
        summed = jnp.dot(sums_ref[d, :rows], band_ref[...], preferred_element_type=F32)
        if not d:
            scale = lax.rsqrt(summed + 1.0)
            for h in range(2):
                for r in range(STRIP):
                    v = scale[r * 16 : (r + 1) * 16, h * 128 : (h + 1) * 128]
                    scale_ref[h, pl.ds(r * XS, 16)] = v
                    scale_ref[h, pl.ds(r * XS + DATES, 8)] = v[:8]
            continue
        for h in range(2):
            for r in range(STRIP):
                both = scale_ref[h, pl.ds(r * XS, 16)] * scale_ref[h, pl.ds(r * XS + d, 16)]
                row = r * 32
                re = summed[row : row + 16, h * 128 : (h + 1) * 128] * both
                im = summed[row + 16 : row + 32, h * 128 : (h + 1) * 128] * both
                re, im = re.astype(BF16).astype(F32), im.astype(BF16).astype(F32)
                base = (d - 1) * 384 + r
                g_ref[h, pl.ds(base, 16, stride=8)] = re
                g_ref[h, pl.ds(base + 128, 16, stride=8)] = re + im
                g_ref[h, pl.ds(base + 256, 16, stride=8)] = im - re


def power_iterations(g_ref, plain, v_ref, c_ref):
    def at(a, b):
        d = (b - a) % DATES
        flip = d > 7
        if flip:
            a, d = b, DATES - d
        return (d - 1) * 384 + a * 8, flip

    def energy(parts):
        total = None
        for re, im in parts:
            term = re * re + im * im
            total = term if total is None else total + term
        return total

    def rescaled(scale, parts):
        return scale * lax.rsqrt(scale * scale * energy(parts) * (1.0 / DATES) + 0.25)

    def half(h, _):
        first = []
        for a in range(DATES):
            re, im = jnp.ones((STRIP, 128), F32), jnp.zeros((STRIP, 128), F32)
            for b in range(DATES):
                if b != a:
                    base, flip = at(a, b)
                    gre = g_ref[h, pl.ds(base, STRIP)]
                    gim = g_ref[h, pl.ds(base + 128, STRIP)] - gre
                    re = re + gre
                    im = im - gim if flip else im + gim
            first.append((re, im))

        def step(_, carry):
            vec, scale = carry
            scale = rescaled(scale, vec)
            both = [re + im for re, im in vec]
            def matvec(a, first, second, ops):
                total = None
                for step in range(1, DATES):
                    b = (a + step) % DATES
                    base, flip = at(a, b)
                    term = g_ref[h, pl.ds(base + (second if flip else first), STRIP)] * ops[b]
                    if total is None:
                        total = term
                    else:
                        total = total - term if flip and first else total + term
                return total

            ones = [matvec(a, 0, 0, both) for a in range(DATES)]
            twos = [ones[a] + matvec(a, 256, 128, [v[0] for v in vec]) for a in range(DATES)]
            out = []
            for a in range(DATES):
                three = matvec(a, 128, 256, [v[1] for v in vec])
                out.append((vec[a][0] + (ones[a] - three), vec[a][1] + twos[a]))
            return tuple(out), scale

        carry = (tuple(first), jnp.ones((STRIP, 128), F32))
        vec, scale = lax.fori_loop(0, ITERS - 1, step, carry, unroll=True)
        scale = rescaled(scale, vec)
        vec = [(re * scale, im * scale) for re, im in vec]
        packed_re, packed_im = None, None
        for t in range(DATES):
            vre, vim = vec[t]
            sre = plain[0, h, pl.ds(t * STRIP * 2, STRIP, stride=2)]
            sim = plain[0, h, pl.ds(t * STRIP * 2 + 1, STRIP, stride=2)]
            re = vre * sre + vim * sim
            im = vre * sim - vim * sre
            packed_re = re if packed_re is None else packed_re + re
            packed_im = im if packed_im is None else packed_im + im
            v_ref[h, pl.ds(t * 8, STRIP)] = vre
            v_ref[h, pl.ds((16 + t) * 8, STRIP)] = vim
        norm = 1.0 / math.sqrt(DATES)
        c_ref[0, h] = packed_re * norm
        c_ref[1, h] = packed_im * norm
        return 0

    lax.fori_loop(0, 2, half, 0)


def main_kernel(
    x_hbm,
    map_hbm,
    out_ref,
    spread_ref,
    map_ref,
    x_ref,
    halo_ref,
    plain,
    x2_ref,
    mid_ref,
    sums_ref,
    band_ref,
    scale_ref,
    g_ref,
    v_ref,
    c_ref,
    pick_ref,
    rows_ref,
    rows2_ref,
    rows3_ref,
    send1,
    recv1,
    sendc,
    recvc,
    send2,
    recv2,
    sem_t,
    sem_x,
    sem_hs,
    sem_hr,
    sem_cs,
    sem_cr,
    sem_1s,
    sem_1r,
    sem_2s,
    sem_2r,
):
    section = lax.axis_index("stack")
    me = lax.axis_index("pix")
    y, rest = lax.div(me, NZ * NC), lax.rem(me, NZ * NC)
    z, c = lax.div(rest, NC), lax.rem(rest, NC)
    other = lax.rem(me + BLOCKS + 2 * c - 1, BLOCKS)

    def at_x(o):
        return {"stack": lax.rem(section + o, SECT)}

    def at_y(o):
        return {"pix": place(lax.rem(y + o, NY), z, c)}

    def at_z(o):
        return {"pix": place(y, lax.rem(z + o, NZ), c)}

    at_core = {"pix": place(y, z, 1 - c)}
    nearest = [
        {"pix": other}, at_core, at_z(1), at_z(NZ - 1), at_y(1), at_y(NY - 1), at_x(1), at_x(SECT - 1)
    ]
    barrier = pltpu.get_barrier_semaphore()
    for peer in nearest:
        pl.semaphore_signal(barrier, inc=1, device_id=peer, device_id_type=MESH)

    def tell(sem, peers):
        for peer in peers:
            pl.semaphore_signal(sem, inc=1, device_id=peer, device_id_type=MESH)

    slots = pltpu.make_async_copy(map_hbm, map_ref, sem_x.at[0])
    slots.start()
    own = pltpu.make_async_copy(x_hbm, x_ref, sem_x.at[1])
    own.start()
    own.wait()
    pl.semaphore_wait(barrier, len(nearest))

    sends = []

    def send(src, dst, ssem, rsem, device):
        copy = pltpu.make_async_remote_copy(
            src_ref=src, dst_ref=dst, send_sem=ssem, recv_sem=rsem,
            device_id=device, device_id_type=MESH,
        )
        copy.start()
        sends.append(copy)
        return copy

    after, before = lax.rem(me + 1, BLOCKS), lax.rem(me + BLOCKS - 1, BLOCKS)
    halos = [
        send(x_ref.at[:, 1:6], halo_ref.at[0], sem_hs.at[0], sem_hr.at[0], {"pix": after}),
        send(x_ref.at[:, 0:5], halo_ref.at[1], sem_hs.at[1], sem_hr.at[1], {"pix": before}),
    ]

    tell(sem_t.at[0], [at_x(1)])
    tell(sem_t.at[1], [at_y(1)])
    tell(sem_t.at[2], [at_z(1), at_z(NZ - 1)])

    g = y * NC + c
    group_of = [lax.rem(g + o, GROUPS) for o in range(GROUPS)]
    groups = [place(lax.div(q, NC), z, lax.rem(q, NC)) for q in group_of]
    far = sorted(range(GROUPS), key=lambda o: -min(o // 2, 4 - o // 2))
    z_of = [lax.rem(z + o, NZ) for o in range(1, NZ)]
    depths = [place(y, q, c) for q in z_of]

    m = iota((128, 128), 0)
    slot = (m >> 5) * 32 + (m & 15) * 2 + ((m >> 4) & 1)
    slots.wait()
    owner = jnp.broadcast_to(map_ref[...], (128, 128))
    chosen = one_hot(slot == owner)
    column = iota((128, 256), 1)
    block = iota((128, 256), 0)
    for k in range(2):
        pick = jnp.dot(chosen, one_hot(column == 2 * block + k), preferred_element_type=F32)
        pick_ref[:, k * 256 : (k + 1) * 256] = pick.astype(BF16)
    band_ref[...] = one_hot(
        jnp.abs((iota((512, 256), 0) & 255) - iota((512, 256), 1)) <= 2
    )
    rows3_ref[...] = jnp.zeros((128, 512), F32)
    for h in range(2):
        for part in range(2):
            v_ref[h, pl.ds((part * 16 + DATES) * 8, 8)] = jnp.zeros((8, 128), F32)

    pl.semaphore_wait(sem_t.at[0], 1)
    pl.semaphore_wait(sem_t.at[1], 1)
    pl.semaphore_wait(sem_t.at[2], 2)
    tell(sem_t.at[3], [at_y(1), at_y(2), at_y(3)])
    tell(sem_t.at[4], [at_z(2), at_z(NZ - 2)])
    unpack(x_ref, plain, 0, STRIP)
    for r in range(STRIP):
        spread(plain, 0, r, UP + r, x2_ref, None)
    middles(x2_ref, mid_ref)
    pl.semaphore_wait(sem_t.at[3], 3)
    pl.semaphore_wait(sem_t.at[4], 2)
    tell(sem_t.at[5], [at_core])
    tell(sem_t.at[6], [at_z(4), at_z(NZ - 4)])
    for copy in halos:
        copy.wait_recv()
    unpack(halo_ref.at[0], plain, 1, UP)
    unpack(halo_ref.at[1], plain, 2, UP)
    for r in range(UP):
        spread(plain, 1, r, r, x2_ref, me > 0)
        spread(plain, 2, r, UP + STRIP + r, x2_ref, me < BLOCKS - 1)
    coherences(x2_ref, mid_ref, sums_ref, band_ref, scale_ref, g_ref)
    power_iterations(g_ref, plain, v_ref, c_ref)
    pl.semaphore_wait(sem_t.at[5], 1)
    pl.semaphore_wait(sem_t.at[6], 2)

    for h in range(2):
        for comp in range(2):
            for k in range(2):
                at = pl.multiple_of(comp * 64 + k * 32 + section * 8, 8)
                lanes = slice(k * 256 + h * 128, k * 256 + (h + 1) * 128)
                rows3_ref[pl.ds(at, STRIP), lanes] = c_ref[comp, h]
    part = lax.dot_general(
        pick_ref[...], rows3_ref[...].astype(BF16), NT_DIMS, preferred_element_type=F32
    ).astype(BF16)
    for q in range(GROUPS):
        sendc[q] = part[q * 16 : (q + 1) * 16]
    def later(s, o):
        return pltpu.make_async_remote_copy(
            src_ref=sendc.at[group_of[o]], dst_ref=recvc.at[section, g],
            send_sem=sem_cs.at[s, o], recv_sem=sem_cr.at[s, o],
            device_id={"stack": section + s, "pix": groups[o]}, device_id_type=MESH,
        )

    for s in (2, 3, 1):

        @pl.when(section + s < SECT)
        def _():
            for o in far:
                later(s, o).start()

    here = [
        send(sendc.at[group_of[o]], recvc.at[section, g], sem_cs.at[0, o], sem_cr.at[0, o], {"pix": groups[o]})
        for o in far
        if o
    ]

    for h in range(2):
        lanes = slice(h * 128, (h + 1) * 128)
        for r in range(4):
            v = v_ref[h, pl.ds(r, FEAT, stride=8)].astype(BF16)
            rows_ref[r * FEAT : (r + 1) * FEAT, lanes] = v
        for r in range(2):
            v = v_ref[h, pl.ds(4 + r, FEAT, stride=8)].astype(BF16)
            for k in range(2):
                at = (k * 2 + r) * FEAT
                rows2_ref[at : at + FEAT, k * 256 + h * 128 : k * 256 + (h + 1) * 128] = v
                rows2_ref[at : at + FEAT, (1 - k) * 256 + h * 128 : (1 - k) * 256 + (h + 1) * 128] = (
                    jnp.zeros((FEAT, 128), BF16)
                )
    for k in range(2):
        part = lax.dot_general(
            pick_ref[:, k * 256 : (k + 1) * 256], rows_ref[...], NT_DIMS, preferred_element_type=F32
        ).astype(BF16)
        for q in range(GROUPS):
            send1[q, :, k * 128 : (k + 1) * 128] = part[q * 16 : (q + 1) * 16]
    part = lax.dot_general(
        pick_ref[...], rows2_ref[...], NT_DIMS, preferred_element_type=F32
    ).astype(BF16)
    for q in range(GROUPS):
        send1[q, :, 256:384] = part[q * 16 : (q + 1) * 16]
    here += [
        send(send1.at[group_of[o]], recv1.at[g], sem_1s.at[o], sem_1r.at[o], {"pix": groups[o]})
        for o in far
        if o
    ]
    recvc[section, g] = sendc[g]
    recv1[g] = send1[g]
    i, j = iota((128, 128), 0), iota((128, 128), 1)
    turn = one_hot(j == (i & 7) * 16 + (i >> 3))
    for copy in here:
        copy.wait_recv()
    for s in range(1, SECT):

        @pl.when(section >= s)
        def _():
            for o in range(GROUPS):
                later(s, o).wait_recv()

    got = recv1[...].reshape(128, 384)
    moved = jnp.dot(turn, got, preferred_element_type=F32)
    for q in range(NZ):
        send2[q, :, :384] = moved[q * 8 : (q + 1) * 8].astype(BF16)
    packed = recvc[0]
    for s in range(1, SECT):
        packed = jnp.where(section >= s, packed + recvc[s], packed)
    packed = packed.reshape(128, 128)
    moved = jnp.dot(turn, packed, preferred_element_type=F32)
    for q in range(NZ):
        send2[q, :, 384:] = moved[q * 8 : (q + 1) * 8].astype(BF16)
    order = sorted(range(NZ - 1), key=lambda o: -min(o + 1, NZ - 1 - o))
    third = [
        send(send2.at[z_of[o]], recv2.at[z], sem_2s.at[o], sem_2r.at[o], {"pix": depths[o]})
        for o in order
    ]
    recv2[z] = send2[z]
    n, lane = iota((128, ROWS), 0), iota((128, ROWS), 1)
    strip = ((n >> 1) & 3) * 32 + (n >> 3) * 2 + (n & 1)
    for r in range(STRIP):
        spread_ref[r * 128 : (r + 1) * 128] = one_hot(lane == strip * STRIP + r)
    for copy in third:
        copy.wait_recv()
    out_ref[...] = recv2[...]
    for copy in sends:
        copy.wait_send()
    for s in range(1, SECT):

        @pl.when(section + s < SECT)
        def _():
            for o in range(GROUPS):
                later(s, o).wait_send()


def run_main(x, owner_map):
    vmem = pl.BlockSpec(memory_space=pltpu.VMEM)
    dma = pltpu.SemaphoreType.DMA
    return pl.pallas_call(
        main_kernel,
        out_shape=(
            jax.ShapeDtypeStruct((NZ, GROUPS, 512), BF16),
            jax.ShapeDtypeStruct((ROWS, ROWS), BF16),
        ),
        in_specs=[pl.BlockSpec(memory_space=pltpu.HBM)] * 2,
        out_specs=(vmem, vmem),
        scratch_shapes=[
            pltpu.VMEM((1, BLOCKS), I32),
            pltpu.VMEM((DATES, STRIP, 2, COLS), BF16),
            pltpu.VMEM((2, DATES, UP, 2, COLS), BF16),
            pltpu.VMEM((3, 2, DATES * STRIP * 2, 128), F32),
            pltpu.VMEM((2, 2, TALL * XS, 128), F32),
            pltpu.VMEM((8, 2, 2, 16, 128), F32),
            pltpu.VMEM((8, STRIP * 32, 512), BF16),
            pltpu.VMEM((512, 256), BF16),
            pltpu.VMEM((2, STRIP * XS, 128), F32),
            pltpu.VMEM((2, 7 * 3 * 128, 128), F32),
            pltpu.VMEM((2, FEAT * 8, 128), F32),
            pltpu.VMEM((2, 2, STRIP, 128), F32),
            pltpu.VMEM((128, 512), BF16),
            pltpu.VMEM((128, 256), BF16),
            pltpu.VMEM((128, 512), BF16),
            pltpu.VMEM((128, 512), F32),
            pltpu.VMEM((GROUPS, NZ, 384), BF16),
            pltpu.VMEM((GROUPS, NZ, 384), BF16),
            pltpu.VMEM((GROUPS, NZ, 128), BF16),
            pltpu.VMEM((SECT, GROUPS, NZ, 128), BF16),
            pltpu.VMEM((NZ, GROUPS, 512), BF16),
            pltpu.VMEM((NZ, GROUPS, 512), BF16),
            pltpu.SemaphoreType.REGULAR((7,)),
            dma((2,)),
            dma((2,)),
            dma((2,)),
            dma((SECT, GROUPS)),
            dma((SECT, GROUPS)),
            dma((GROUPS,)),
            dma((GROUPS,)),
            dma((NZ - 1,)),
            dma((NZ - 1,)),
        ],
        compiler_params=pltpu.CompilerParams(
            collective_id=0, has_side_effects=True, vmem_limit_bytes=20 * 1024 * 1024
        ),
        name="link",
    )(x, owner_map)


def finish_kernel(got_ref, spread_ref, linked_ref, compressed_ref, turned_ref):
    section = lax.axis_index("stack")
    got = jnp.concatenate([got_ref[q].astype(F32) for q in range(NZ)], axis=0)
    for tile in range(4):
        turned_ref[tile * 128 : (tile + 1) * 128] = got[:, tile * 128 : (tile + 1) * 128].T
    blocks = []
    for k in range(2):
        pieces = []
        for r in range(STRIP):
            at = k * 128 + r * FEAT if r < 4 else 256 + (k * 2 + r - 4) * FEAT
            pieces.append(turned_ref[pl.ds(at, FEAT)].astype(BF16))
        blocks.append(jnp.concatenate(pieces, axis=1))
    pieces = []
    for r in range(STRIP):
        pair = [turned_ref[pl.ds(384 + comp * 64 + r, 8, stride=8)] for comp in range(2)]
        pieces.append(jnp.concatenate(pair, axis=0).astype(BF16))
    blocks.append(jnp.concatenate(pieces, axis=1))
    out = jnp.dot(jnp.concatenate(blocks, axis=0), spread_ref[...], preferred_element_type=F32)
    re, im = out[64:72], out[72:80]
    link_re = re[1:] * re[:-1] + im[1:] * im[:-1]
    link_im = im[1:] * re[:-1] - re[1:] * im[:-1]
    factor = lax.rsqrt(link_re * link_re + link_im * link_im + 1.0)
    unit_re, unit_im = link_re * factor, link_im * factor
    tiles = ROWS // 128
    for k in range(2):
        datum_re, datum_im = jnp.ones((1, ROWS), F32), jnp.zeros((1, ROWS), F32)
        mine_re, mine_im = re[k * 4 : k * 4 + 1], im[k * 4 : k * 4 + 1]
        for j in range(SECT - 1):
            at = k * 4 + j
            ure, uim = unit_re[at : at + 1], unit_im[at : at + 1]
            new_re = datum_re * ure - datum_im * uim
            new_im = datum_re * uim + datum_im * ure
            reached = j < section
            datum_re = jnp.where(reached, new_re, datum_re)
            datum_im = jnp.where(reached, new_im, datum_im)
            mine_re = jnp.where(reached, re[at + 1 : at + 2], mine_re)
            mine_im = jnp.where(reached, im[at + 1 : at + 2], mine_im)
        at = k * FEAT
        vre, vim = out[at : at + DATES], out[at + 16 : at + 16 + DATES]
        linked = (vre * datum_re - vim * datum_im, vre * datum_im + vim * datum_re)
        mine = (mine_re, mine_im)
        for part in range(2):
            for tile in range(tiles):
                row = part * DATES * 2 * tiles + k * tiles + tile
                lanes = slice(tile * 128, (tile + 1) * 128)
                linked_ref[pl.ds(row, DATES, stride=2 * tiles)] = linked[part][:, lanes]
                row = part * 2 * tiles + k * tiles + tile
                compressed_ref[pl.ds(row, 1)] = mine[part][:, lanes]


def run_finish(got, spread):
    vmem = pl.BlockSpec(memory_space=pltpu.VMEM)
    return pl.pallas_call(
        finish_kernel,
        out_shape=(
            jax.ShapeDtypeStruct((2 * DATES * 12, 128), F32),
            jax.ShapeDtypeStruct((24, 128), F32),
        ),
        in_specs=[vmem, vmem],
        out_specs=(vmem, vmem),
        scratch_shapes=[pltpu.VMEM((512, 128), F32)],
        compiler_params=pltpu.CompilerParams(vmem_limit_bytes=20 * 1024 * 1024),
        name="finish",
    )(got, spread)


def local(slc, owner_map):
    x = jnp.transpose(slc[:, 0], (1, 2, 0, 3))
    linked, compressed = run_finish(*run_main(pltpu.with_memory_space_constraint(x, pltpu.HBM), pltpu.with_memory_space_constraint(owner_map.reshape(1, BLOCKS), pltpu.HBM)))
    return (
        linked.reshape(2, 1, DATES, 1, 2 * ROWS),
        compressed.reshape(2, 1, 1, 2 * ROWS),
    )


def solution(mesh):
    in_specs = (P(None, "stack", None, "pix", None), P())
    out_specs = (P(None, "stack", None, "pix", None), P(None, "stack", "pix", None))
    return jax.shard_map(local, mesh=mesh, in_specs=in_specs, out_specs=out_specs, check_vma=False)
```
